128 devices in a mesh: task: 8 (over z, core), mp: 16 (over y, x).
Axes of the slice: x: 4, y: 4, z: 4, core: 2. Of those that a mesh axis runs over, the one named last changes fastest.
Arguments:
- deter: float32 [2048, 4096], P('task', 'mp'), may hold values from -3 to 3
- draws: int32 [4, 32, 2048], P(None, None, 'task'), may hold values from 0 to 31
- actions: int32 [4, 2048], P(None, 'task'), may hold values from 0 to 17
- horizons: int32 [64], replicated, may hold values from 5 to 30, as said below
- offsets: int32 [4, 4], replicated, may hold values from 0 to 7, as said below
- embed_stoch: bfloat16 [1024, 1024], replicated, may hold values from -1 to 1
- embed_act: bfloat16 [18, 1024], replicated, may hold values from -6 to 6
- gru_weight: bfloat16 [5120, 3, 4096], P(None, None, 'mp'), may hold values from -0.078125 to 0.078125
- prior_weight: bfloat16 [4096, 1024], replicated, may hold values from -0.09375 to 0.09375
- logit_weight: bfloat16 [1024, 1024], replicated, may hold values from -0.75 to 0.75
- head_weight: bfloat16 [1024, 2], replicated, may hold values from -0.375 to 0.375
Outputs:
- log_prob: float32 [4, 2048], P(None, 'task')
- reward: float32 [4, 2048], P(None, 'task')
- continuation: float32 [4, 2048], P(None, 'task')
- final_deter: float32 [2048, 4096], P('task', 'mp')
The draws below stay inside these ranges and needn't reach their ends.
Inputs may be any that keep to these rules, and one draw needn't show every extreme that they name: `horizons`: rows of task k are home rows k * (32) up to (k + 1) * 32 - 1. `offsets`: the 4 numbers of one row are distinct.
All inputs are finite; a program needn't handle non-finite values.
Results may differ from the reference program's by a relative error of at most 0.0045.
Values may be sent and summed in bfloat16 or wider, within the bound.
No kernel may reach another device: no remote copies, remote signals or barrier semaphores. Data moves between devices by JAX's collectives and lax.ppermute only.
A program may use at most 128 MiB of HBM per device.

```python
import jax
import jax.numpy as jnp
from jax import lax

DET = 4096
HID = 1024
GROUPS = 32
CLASSES = 32
ACTS = 18
TASKS = 64
BLK_DEV = 4
BROWS = 64
STEPS = 4
WSTART = 16
STOCH = 1024
BLOCKS = 32
ROWS = 2048
N_TASK = 8


def plan_helper(key):
    horizon_key = jax.random.fold_in(key, 11)
    horizons = jax.random.randint(horizon_key, (TASKS,), 5, 31).astype(jnp.int32)
    holders = BLOCKS // BLK_DEV
    per_task = BLOCKS * BROWS // TASKS
    row_task = jnp.arange(BLOCKS * BROWS, dtype=jnp.int32) // per_task
    places = jnp.arange(holders, dtype=jnp.int32)[:, None]
    local_slot = jnp.arange(BLK_DEV, dtype=jnp.int32)[None, :]
    running = jnp.zeros((BLK_DEV,), jnp.int32)
    shift_rows = []
    for moment in range(STEPS):
        live_rows = (horizons[row_task] > WSTART + moment).astype(jnp.int32)
        live_blocks = jnp.max(live_rows.reshape(BLOCKS, BROWS), axis=1).reshape(holders, BLK_DEV)
        moment_key = jax.random.fold_in(jax.random.fold_in(key, 23), moment)
        candidates = []
        heaviest = []
        for option in range(16):
            shifts = jax.random.permutation(jax.random.fold_in(moment_key, option), holders)[:BLK_DEV].astype(jnp.int32)
            landing = (running + shifts) % holders
            source = (places - landing[None, :]) % holders
            slot_live = live_blocks[source, local_slot]
            heaviest.append(jnp.max(jnp.sum(slot_live, axis=1)))
            candidates.append(shifts)
        chosen = jnp.argmin(jnp.stack(heaviest))
        shifts = jnp.stack(candidates)[chosen]
        running = (running + shifts) % holders
        shift_rows.append(shifts)
    return (horizons, jnp.stack(shift_rows).astype(jnp.int32))


def draw_horizons(key, part):
    return plan_helper(key)[0]


def draw_offsets(key, part):
    return plan_helper(key)[1]


def set_ends(array, stream_key, smallest, high):
    shape = array.shape
    index_at = [jax.random.randint(jax.random.fold_in(stream_key, axis), (), 0, shape[axis]) for axis in range(len(shape))]
    array = array.at[tuple(index_at)].set(smallest)
    longest = shape.index(max(shape))
    index_at[longest] = (index_at[longest] + 1) % shape[longest]
    return array.at[tuple(index_at)].set(high)


def level_of(stream_key, dims, pieces, smallest, high):
    factor_of = 1.0
    for axis_at, blocks in pieces:
        steps = jax.random.uniform(jax.random.fold_in(jax.random.fold_in(stream_key, 6), axis_at), (blocks,), jnp.float32, smallest / len(pieces), high / len(pieces))
        factor_of = factor_of * jnp.repeat(jnp.exp(steps), dims[axis_at] // blocks).reshape((-1,) + (1,) * (len(dims) - 1 - axis_at))
    return factor_of


def normal_values(stream_key, shape, deviation, limit, cuts=(), held_as=jnp.bfloat16):
    factor_of = level_of(stream_key, shape, cuts, -0.22, 0.18) if cuts else 1.0
    values = jax.random.normal(stream_key, shape, jnp.float32) * deviation * factor_of
    return jnp.minimum(jnp.maximum(values, -limit), limit).astype(held_as)


def setup_inputs(seed: int = 0) -> dict:
    arg_keys = jax.random.split(jax.random.key(seed), 12)
    deter = normal_values(arg_keys[0], (ROWS, DET), 0.5, 3.0, ((0, 8), (1, 16)), jnp.float32)
    draws = set_ends(jax.random.randint(arg_keys[1], (STEPS, GROUPS, ROWS), 0, CLASSES), jax.random.fold_in(arg_keys[1], 1), 0, CLASSES - 1).astype(jnp.int32)
    actions = set_ends(jax.random.randint(arg_keys[2], (STEPS, ROWS), 0, ACTS), jax.random.fold_in(arg_keys[2], 1), 0, ACTS - 1).astype(jnp.int32)
    horizons = draw_horizons(jax.random.fold_in(arg_keys[11], 71), 0)
    offsets = draw_offsets(jax.random.fold_in(arg_keys[11], 71), 0)
    embed_stoch = normal_values(arg_keys[5], (STOCH, HID), GROUPS ** -0.5, 1.0)
    embed_act = normal_values(arg_keys[6], (ACTS, HID), 1.0, 6.0)
    gru_weight = normal_values(arg_keys[7], (HID + DET, 3, DET), (HID + DET) ** -0.5, 0.078125, ((2, 16),))
    prior_weight = normal_values(arg_keys[8], (DET, HID), DET ** -0.5, 0.09375)
    logit_weight = normal_values(arg_keys[9], (HID, STOCH), (HID // 16) ** -0.5, 0.75)
    head_weight = normal_values(arg_keys[10], (HID, 2), (HID // 4) ** -0.5, 0.375)
    return {"deter": deter, "draws": draws, "actions": actions, "horizons": horizons, "offsets": offsets, "embed_stoch": embed_stoch, "embed_act": embed_act, "gru_weight": gru_weight, "prior_weight": prior_weight, "logit_weight": logit_weight, "head_weight": head_weight}


def layer_norm(values):
    average = lax.optimization_barrier(jnp.mean(values, axis=-1, keepdims=True))
    squares = lax.optimization_barrier(jnp.mean(values * values, axis=-1, keepdims=True))
    return (values - average) * lax.rsqrt(squares - average * average + 1e-05)

def reference(deter, draws, actions, horizons, offsets, embed_stoch, embed_act, gru_weight, prior_weight, logit_weight, head_weight):
    rows_total = deter.shape[0]
    per_task = rows_total // TASKS
    holders = N_TASK
    places = jnp.arange(holders, dtype=jnp.int32)[:, None]
    local_slot = jnp.arange(BLK_DEV, dtype=jnp.int32)[None, :]
    within = jnp.arange(BROWS, dtype=jnp.int32)
    classes = jnp.arange(CLASSES, dtype=jnp.int32)
    action_ids = jnp.arange(ACTS, dtype=jnp.int32)
    gate_matrix = gru_weight.reshape(HID + DET, 3 * DET)
    carried = deter
    running = jnp.zeros((BLK_DEV,), jnp.int32)
    logp_list, reward_list, cont_list = ([], [], [])
    for moment in range(STEPS):
        offset_now = offsets[moment].astype(jnp.int32)
        source = ((places - offset_now[None, :]) % holders).astype(jnp.int32)
        carried = carried.reshape(holders, BLK_DEV, BROWS, DET)[source, local_slot].reshape(rows_total, DET)
        running = (running + offset_now) % holders
        home_block = (places - running[None, :]) % holders * BLK_DEV + local_slot
        home_rows = (home_block[:, :, None] * BROWS + within).reshape(rows_total).astype(jnp.int32)
        living = (horizons[home_rows // per_task] > WSTART + moment).astype(jnp.float32)
        chosen_hot = (jnp.transpose(draws[moment])[:, :, None] == classes).astype(jnp.float32)
        stoch_hot = chosen_hot.astype(jnp.bfloat16).reshape(rows_total, STOCH)
        action_hot = (actions[moment][:, None] == action_ids[None, :]).astype(jnp.bfloat16)
        carried_low = carried.astype(jnp.bfloat16)
        embed_pre = jnp.dot(stoch_hot, embed_stoch, preferred_element_type=jnp.float32) + jnp.dot(action_hot, embed_act, preferred_element_type=jnp.float32)
        embedded = jax.nn.silu(layer_norm(embed_pre)).astype(jnp.bfloat16)
        joined = jnp.concatenate([embedded, carried_low], axis=1)
        gate_parts = jnp.dot(joined, gate_matrix, preferred_element_type=jnp.float32)
        normed = layer_norm(gate_parts).reshape(rows_total, 3, DET)
        reset_gate = jax.nn.sigmoid(normed[:, 0])
        candidate = jnp.tanh(reset_gate * normed[:, 1])
        update = jax.nn.sigmoid(normed[:, 2] - 1.0)
        renewed = update * candidate + (1.0 - update) * carried
        prior_pre = jnp.dot(carried_low, prior_weight, preferred_element_type=jnp.float32)
        hidden = jax.nn.silu(layer_norm(prior_pre)).astype(jnp.bfloat16)
        raw_logits = jnp.dot(hidden, logit_weight, preferred_element_type=jnp.float32).reshape(rows_total, GROUPS, CLASSES)
        capped = 5.0 * jnp.tanh(raw_logits / 5.0)
        exponent = jnp.exp(capped)
        chances = 0.99 * exponent / lax.optimization_barrier(jnp.sum(exponent, axis=-1, keepdims=True)) + 0.01 / CLASSES
        log_prob = lax.optimization_barrier(jnp.sum(jnp.log(lax.optimization_barrier(jnp.sum(chances * chosen_hot, axis=-1))), axis=-1)) * living
        head_out = jnp.dot(hidden, head_weight, preferred_element_type=jnp.float32)
        logp_list.append(log_prob)
        reward_list.append(head_out[:, 0] * living)
        cont_list.append(jax.nn.sigmoid(head_out[:, 1]) * living)
        carried = jnp.where(living[:, None] > 0, renewed, carried)
    return (jnp.stack(logp_list), jnp.stack(reward_list), jnp.stack(cont_list), carried)
```

```python
import functools

import jax
import jax.numpy as jnp
from jax import lax
from jax.experimental import pallas as pl
from jax.experimental.pallas import tpu as pltpu
from jax.sharding import PartitionSpec as P

HID = 1024
GROUPS = 32
CLASSES = 32
TASKS = 64
BLK_DEV = 4
STEPS = 4
WSTART = 16
ACT_PAD = 32
VMEM_LIMIT = 48 * 1024 * 1024
F32 = jnp.float32
BF16 = jnp.bfloat16


def silu(v):
    return v / (1.0 + jnp.exp(-v))


def sigmoid(v):
    return 1.0 / (1.0 + jnp.exp(-v))


def row_norm(pre):
    entries = pre.shape[1]
    avg = jnp.sum(pre, axis=1, keepdims=True) / entries
    squares = jnp.sum(pre * pre, axis=1, keepdims=True) / entries
    return (pre - avg) * lax.rsqrt(squares - avg * avg + 1e-5)


def spread_matrix():
    variable = lax.broadcasted_iota(jnp.int32, (GROUPS, HID), 0)
    entry = lax.broadcasted_iota(jnp.int32, (GROUPS, HID), 1)
    return (entry // CLASSES == variable).astype(BF16)


def chosen_mask(draw_rows, spread):
    by_row = jnp.transpose(draw_rows).astype(BF16)
    wide = jnp.dot(by_row, spread, preferred_element_type=F32)
    entry = lax.broadcasted_iota(jnp.int32, wide.shape, 1)
    return wide == (entry % CLASSES).astype(F32)


def embed_kernel(draw_ref, stoch_ref, act_ref, out_ref):
    picks = draw_ref[0].astype(F32)
    rows = picks.shape[1]
    hot = chosen_mask(picks[:GROUPS], spread_matrix()).astype(F32).astype(BF16)
    action = picks[GROUPS : GROUPS + 1]
    ids = lax.broadcasted_iota(jnp.int32, (ACT_PAD, rows), 0).astype(F32)
    act_hot = jnp.transpose((ids == action).astype(F32)).astype(BF16)
    pre = jnp.dot(hot, stoch_ref[...], preferred_element_type=F32) + jnp.dot(
        act_hot, act_ref[...], preferred_element_type=F32
    )
    out_ref[0] = silu(row_norm(pre)).astype(BF16)


def gates_kernel(chunks, emb_ref, x_ref, w_ref, g_ref, stat_ref, acc_ref):
    step = pl.program_id(0)

    @pl.when(step == 0)
    def _():
        acc_ref[...] = jnp.dot(emb_ref[...], w_ref[...], preferred_element_type=F32)

    @pl.when(step > 0)
    def _():
        left = jnp.concatenate([x_ref[q] for q in range(x_ref.shape[0])], axis=1)
        acc_ref[...] += jnp.dot(left, w_ref[...], preferred_element_type=F32)

    @pl.when(step == chunks - 1)
    def _():
        total = acc_ref[...]
        g_ref[...] = total
        part = total[:, :128]
        part_sq = part * part
        for q in range(1, total.shape[1] // 128):
            piece = total[:, q * 128 : (q + 1) * 128]
            part += piece
            part_sq += piece * piece
        sums = jnp.concatenate(
            [
                jnp.sum(jnp.transpose(part), axis=0, keepdims=True),
                jnp.sum(jnp.transpose(part_sq), axis=0, keepdims=True),
            ],
            axis=0,
        )
        for q in range(stat_ref.shape[0]):
            stat_ref[q] = sums


def lanes_from_row(row):
    return jnp.transpose(jnp.broadcast_to(row, (128, row.shape[1])))


def update_kernel(entries, g_ref, stat_ref, carried_ref, live_ref, new_ref, low_ref):
    sums = jnp.sum(stat_ref[...], axis=0) / entries
    avg = sums[0:1]
    inv = lax.rsqrt(sums[1:2] - avg * avg + 1e-5)
    avg_l = lanes_from_row(avg)
    inv_l = lanes_from_row(inv)
    live_l = lanes_from_row(live_ref[...])
    share = carried_ref.shape[1]
    for q in range(share // 128):
        def normed(part):
            at = part * share + q * 128
            return (g_ref[:, at : at + 128] - avg_l) * inv_l

        held = carried_ref[:, q * 128 : (q + 1) * 128]
        reset = sigmoid(normed(0))
        candidate = jnp.tanh(reset * normed(1))
        update = sigmoid(normed(2) - 1.0)
        renewed = update * candidate + (1.0 - update) * held
        renewed = jnp.where(live_l > 0, renewed, held)
        new_ref[:, q * 128 : (q + 1) * 128] = renewed
        low = renewed.astype(BF16)
        for k in range(low_ref.shape[0]):
            low_ref[k, :, q * 128 : (q + 1) * 128] = low


def two_parts(values):
    high = values.astype(BF16)
    return high, (values - high.astype(F32)).astype(BF16)


def over_groups(spread, values):
    dims = (((1,), (1,)), ((), ()))
    high, rest = two_parts(values)
    return lax.dot_general(spread, high, dims, preferred_element_type=F32) + lax.dot_general(
        spread, rest, dims, preferred_element_type=F32
    )


def prior_kernel(chunks, x_ref, w_ref, logit_ref, head_ref, draw_ref, live_ref, out_ref, acc_ref):
    step = pl.program_id(0)
    left = jnp.concatenate([x_ref[q] for q in range(x_ref.shape[0])], axis=1)
    part = jnp.dot(left, w_ref[...], preferred_element_type=F32)

    @pl.when(step == 0)
    def _():
        acc_ref[...] = part

    @pl.when(step > 0)
    def _():
        acc_ref[...] += part

    @pl.when(step == chunks - 1)
    def _():
        hidden = silu(row_norm(acc_ref[...])).astype(BF16)
        heads = lax.dot_general(
            head_ref[...], hidden, (((1,), (1,)), ((), ())), preferred_element_type=F32
        )
        raw = jnp.dot(hidden, logit_ref[...], preferred_element_type=F32)
        exponent = jnp.exp(5.0 * jnp.tanh(raw / 5.0))
        spread = spread_matrix()
        chosen = jnp.where(chosen_mask(draw_ref[0, :GROUPS].astype(F32), spread), exponent, 0.0)
        chances = 0.99 * over_groups(spread, chosen) / over_groups(spread, exponent) + 0.01 / CLASSES
        log_prob = jnp.sum(jnp.log(chances), axis=0, keepdims=True)
        live = live_ref[...]
        out_ref[...] = jnp.concatenate(
            [
                log_prob * live,
                heads[0:1] * live,
                sigmoid(heads[1:2]) * live,
                jnp.zeros((5, live.shape[1]), F32),
            ],
            axis=0,
        )


def params():
    return pltpu.CompilerParams(vmem_limit_bytes=VMEM_LIMIT)


def embed_all(picks, stoch, act):
    steps, depth, rows = picks.shape
    return pl.pallas_call(
        embed_kernel,
        grid=(steps,),
        in_specs=[
            pl.BlockSpec((1, depth, rows), lambda t: (t, 0, 0)),
            pl.BlockSpec(stoch.shape, lambda t: (0, 0)),
            pl.BlockSpec(act.shape, lambda t: (0, 0)),
        ],
        out_specs=pl.BlockSpec((1, rows, HID), lambda t: (t, 0, 0)),
        out_shape=jax.ShapeDtypeStruct((steps, rows, HID), BF16),
        compiler_params=params(),
        name="embed",
    )(picks, stoch, act)


def gates(emb, x, w):
    shards, rows, share = x.shape
    per = HID // share
    chunks = 1 + shards // per
    width = w.shape[1]
    return pl.pallas_call(
        functools.partial(gates_kernel, chunks),
        grid=(chunks,),
        in_specs=[
            pl.BlockSpec((rows, HID), lambda i: (0, 0)),
            pl.BlockSpec((per, rows, share), lambda i: (jnp.maximum(i - 1, 0), 0, 0)),
            pl.BlockSpec((HID, width), lambda i: (i, 0)),
        ],
        out_specs=[
            pl.BlockSpec((rows, width), lambda i: (0, 0)),
            pl.BlockSpec((shards, 2, rows), lambda i: (0, 0, 0)),
        ],
        out_shape=[
            jax.ShapeDtypeStruct((rows, width), F32),
            jax.ShapeDtypeStruct((shards, 2, rows), F32),
        ],
        scratch_shapes=[pltpu.VMEM((rows, width), F32)],
        compiler_params=params(),
        name="gates",
    )(emb, x, w)


def renew(g, stats, carried, live, entries):
    shards = stats.shape[0]
    rows, share = carried.shape
    return pl.pallas_call(
        functools.partial(update_kernel, entries),
        out_shape=[
            jax.ShapeDtypeStruct((rows, share), F32),
            jax.ShapeDtypeStruct((shards, rows, share), BF16),
        ],
        compiler_params=params(),
        name="renew",
    )(g, stats, carried, live)


def prior(x, w, logit, head, picks, live, moment):
    shards, rows, share = x.shape
    per = HID // share
    chunks = shards // per
    depth = picks.shape[1]
    return pl.pallas_call(
        functools.partial(prior_kernel, chunks),
        grid=(chunks,),
        in_specs=[
            pl.BlockSpec((per, rows, share), lambda i: (i, 0, 0)),
            pl.BlockSpec((HID, HID), lambda i: (i, 0)),
            pl.BlockSpec((HID, HID), lambda i: (0, 0)),
            pl.BlockSpec(head.shape, lambda i: (0, 0)),
            pl.BlockSpec((1, depth, rows), lambda i: (moment, 0, 0)),
            pl.BlockSpec((1, rows), lambda i: (0, 0)),
        ],
        out_specs=pl.BlockSpec((8, rows), lambda i: (0, 0)),
        out_shape=jax.ShapeDtypeStruct((8, rows), F32),
        scratch_shapes=[pltpu.VMEM((rows, HID), F32)],
        compiler_params=params(),
        name="prior",
    )(x, w, logit, head, picks, live)


def exchange(copies, axis):
    return lax.all_to_all(copies, axis, 0, 0, tiled=True)


def on_device(
    deter,
    draws,
    actions,
    horizons,
    offsets,
    embed_stoch,
    embed_act,
    gru_weight,
    prior_weight,
    logit_weight,
    head_weight,
):
    holders = lax.axis_size("task")
    place = lax.axis_index("task")
    shards = lax.axis_size("mp")
    rows, share = deter.shape
    block = rows // BLK_DEV
    per_task = rows * holders // TASKS
    entries = 3 * share * shards
    gate_matrix = gru_weight.reshape(gru_weight.shape[0], 3 * share)
    act_table = jnp.pad(embed_act, ((0, ACT_PAD - embed_act.shape[0]), (0, 0)))
    head_rows = jnp.pad(jnp.transpose(head_weight), ((0, 6), (0, 0)))
    low = deter.astype(BF16)
    x = exchange(jnp.broadcast_to(low[None], (shards, rows, share)), "mp")

    depth = 40
    sent = jnp.concatenate(
        [draws, actions[:, None], jnp.zeros((STEPS, depth - GROUPS - 1, rows), jnp.int32)], axis=1
    ).astype(BF16)
    everyone = lax.all_gather(sent, "task")
    running = jnp.cumsum(offsets, axis=0) % holders
    slots = (place + running) % holders
    places = jnp.arange(holders, dtype=jnp.int32)
    taking = (slots[None] == places[:, None, None]).astype(BF16)
    picks = jnp.sum(
        everyone.reshape(holders, STEPS, depth, BLK_DEV, block) * taking[:, :, None, :, None],
        axis=0,
        dtype=BF16,
    ).reshape(STEPS, depth, rows)

    task_of_row = place * (rows // per_task) + jnp.arange(rows, dtype=jnp.int32) // per_task
    horizon = jnp.sum(
        jnp.where(
            task_of_row[None, :] == jnp.arange(TASKS, dtype=jnp.int32)[:, None],
            horizons[:, None],
            0,
        ),
        axis=0,
    )
    moments = WSTART + jnp.arange(STEPS, dtype=jnp.int32)
    living = (horizon[None, :] > moments[:, None]).astype(F32)

    embedded = embed_all(picks, embed_stoch, act_table)
    carried = deter
    small = []
    for moment in range(STEPS):
        live = living[moment : moment + 1]
        g, stats = gates(embedded[moment], x, gate_matrix)
        stats = exchange(stats, "mp")
        small.append(prior(x, prior_weight, logit_weight, head_rows, picks, live, moment))
        carried, low = renew(g, stats, carried, live, entries)
        if moment < STEPS - 1:
            x = exchange(low, "mp")

    outs = lax.all_gather(jnp.stack(small)[:, :3], "task")
    source = (place - running) % holders
    giving = (source[None] == places[:, None, None]).astype(F32)
    outs = jnp.sum(
        outs.reshape(holders, STEPS, 3, BLK_DEV, block) * giving[:, :, None, :, None], axis=0
    ).reshape(STEPS, 3, rows)
    states = lax.all_gather(low[0], "task").reshape(holders, BLK_DEV, block, share)
    final = jnp.concatenate(
        [
            lax.dynamic_slice(states, (source[STEPS - 1, j], j, 0, 0), (1, 1, block, share))[0, 0]
            for j in range(BLK_DEV)
        ],
        axis=0,
    ).astype(F32)
    return (outs[:, 0], outs[:, 1], outs[:, 2], final)


def solution(mesh):
    in_specs = (
        P("task", "mp"),
        P(None, None, "task"),
        P(None, "task"),
        P(),
        P(),
        P(),
        P(),
        P(None, None, "mp"),
        P(),
        P(),
        P(),
    )
    out_specs = (P(None, "task"), P(None, "task"), P(None, "task"), P("task", "mp"))
    return jax.shard_map(
        on_device, mesh=mesh, in_specs=in_specs, out_specs=out_specs, check_vma=False
    )
```

```python
import functools

import jax
import jax.numpy as jnp
from jax import lax
from jax.experimental import pallas as pl
from jax.experimental.pallas import tpu as pltpu
from jax.sharding import PartitionSpec as P

HID = 1024
GROUPS = 32
CLASSES = 32
TASKS = 64
BLK_DEV = 4
STEPS = 4
WSTART = 16
ACT_PAD = 32
DEPTH = 40
LEVELS = (5, 6, 8)
PIECE = 32
F32 = jnp.float32
BF16 = jnp.bfloat16
I32 = jnp.int32


def silu(v):
    return v / (1.0 + jnp.exp(-v))


def sigmoid(v):
    return 1.0 / (1.0 + jnp.exp(-v))


def row_norm(pre):
    entries = pre.shape[1]
    avg = jnp.sum(pre, axis=1, keepdims=True) / entries
    squares = jnp.sum(pre * pre, axis=1, keepdims=True) / entries
    return (pre - avg) * lax.rsqrt(squares - avg * avg + 1e-5)


def spread_matrix():
    variable = lax.broadcasted_iota(I32, (GROUPS, HID), 0)
    entry = lax.broadcasted_iota(I32, (GROUPS, HID), 1)
    return (entry // CLASSES == variable).astype(F32).astype(BF16)


def chosen_mask(by_row, spread):
    wide = jnp.dot(by_row, spread, preferred_element_type=F32)
    entry = lax.broadcasted_iota(I32, wide.shape, 1)
    return wide == (entry % CLASSES).astype(F32)


def selector(length, at):
    place = lax.broadcasted_iota(I32, (length, at.shape[1]), 0)
    return (place == at).astype(F32).astype(BF16)


def side_by_side(ref):
    return jnp.concatenate([ref[q] for q in range(ref.shape[0])], axis=1)


def embed_kernel(at_ref, ev_ref, stoch_ref, act_ref, *refs):
    steps = ev_ref.shape[0]
    outs, all_picks, (hot_ref, pre_ref) = refs[:steps], refs[steps : 2 * steps], refs[2 * steps :]
    rows = pre_ref.shape[0]
    spread = spread_matrix()
    ids = lax.broadcasted_iota(I32, (PIECE, ACT_PAD), 1).astype(F32)
    for step in range(steps):
        picks_ref, out_ref = all_picks[step], outs[step]

        def mark(k, _, step=step, picks_ref=picks_ref):
            at = pl.ds(pl.multiple_of(k * PIECE, PIECE), PIECE)
            wanted = ev_ref[step, pl.ds(pl.multiple_of(at_ref[step, k], PIECE), PIECE)]
            picks_ref[at] = wanted
            hot_ref[at, :HID] = chosen_mask(wanted[:, :GROUPS], spread).astype(F32).astype(BF16)
            action = wanted[:, GROUPS : GROUPS + 1].astype(F32)
            hot_ref[at, HID:] = (ids == action).astype(F32).astype(BF16)
            return 0

        lax.fori_loop(0, rows // PIECE, mark, 0)
        pre_ref[...] = jnp.dot(
            hot_ref[:, :HID], stoch_ref[...], preferred_element_type=F32
        ) + jnp.dot(hot_ref[:, HID:], act_ref[...], preferred_element_type=F32)

        def finish(k, _, out_ref=out_ref):
            at = pl.ds(pl.multiple_of(k * PIECE, PIECE), PIECE)
            out_ref[at] = silu(row_norm(pre_ref[at])).astype(BF16)
            return 0

        lax.fori_loop(0, rows // PIECE, finish, 0)


def full_lanes(part):
    rows = part.shape[0]
    if rows < 256:
        part = jnp.concatenate([part, jnp.zeros((256 - rows, 128), F32)], axis=0)
    return jnp.transpose(part)


def lanes_from_row(row, rows):
    return jnp.transpose(jnp.broadcast_to(row, (128, row.shape[1])))[:rows]


def gates_kernel(emb_ref, x_ref, w_ref, g_ref, stat_ref, wbuf, sem):
    parts, depth, share = w_ref.shape
    chunks = depth // HID

    def fetch(c):
        at = pl.ds(pl.multiple_of(c * HID, HID), HID)
        return pltpu.make_async_copy(w_ref.at[:, at, :], wbuf.at[c], sem.at[c])

    for c in range(chunks):
        fetch(c).start()
    per = HID // share
    fetch(0).wait()
    for k in range(parts):
        g_ref[:, k * share : (k + 1) * share] = jnp.dot(
            emb_ref[...], wbuf[0, k], preferred_element_type=F32
        )

    def add(c, _):
        left = jnp.concatenate([x_ref[(c - 1) * per + q] for q in range(per)], axis=1)
        fetch(c).wait()
        for k in range(parts):
            g_ref[:, k * share : (k + 1) * share] += jnp.dot(
                left, wbuf[c, k], preferred_element_type=F32
            )
        return 0

    lax.fori_loop(1, chunks, add, 0)
    rows, width = g_ref.shape
    part = jnp.zeros((rows, 128), F32)
    part_sq = part
    for q in range(width // 128):
        piece = g_ref[:, q * 128 : (q + 1) * 128]
        part += piece
        part_sq += piece * piece
    sums = jnp.concatenate(
        [
            jnp.sum(full_lanes(part), axis=0, keepdims=True),
            jnp.sum(full_lanes(part_sq), axis=0, keepdims=True),
        ],
        axis=0,
    )
    for q in range(stat_ref.shape[0]):
        stat_ref[q] = sums


def update_kernel(entries, g_ref, stat_ref, carried_ref, live_ref, new_ref, low_ref):
    sums = jnp.sum(stat_ref[...], axis=0) / entries
    avg = sums[0:1]
    inv = lax.rsqrt(sums[1:2] - avg * avg + 1e-5)
    rows, share = carried_ref.shape
    avg_l = lanes_from_row(avg, rows)
    inv_l = lanes_from_row(inv, rows)
    live_l = lanes_from_row(live_ref[...], rows)
    for q in range(share // 128):
        def normed(part):
            at = part * share + q * 128
            return (g_ref[:, at : at + 128] - avg_l) * inv_l

        held = carried_ref[:, q * 128 : (q + 1) * 128]
        reset = sigmoid(normed(0))
        candidate = jnp.tanh(reset * normed(1))
        update = sigmoid(normed(2) - 1.0)
        renewed = update * candidate + (1.0 - update) * held
        renewed = jnp.where(live_l > 0, renewed, held)
        new_ref[:, q * 128 : (q + 1) * 128] = renewed
        low = renewed.astype(BF16)
        for k in range(low_ref.shape[0]):
            low_ref[k, :, q * 128 : (q + 1) * 128] = low


def two_parts(values):
    high = values.astype(BF16)
    return high, (values - high.astype(F32)).astype(BF16)


def prior_kernel(
    x_ref, w_ref, logit_ref, head_ref, picks_ref, live_ref, out_ref,
    wbuf, lbuf, pre_ref, hid_ref, parts_ref, sem,
):
    shards, rows, share = x_ref.shape
    chunks = w_ref.shape[0] // HID
    per = HID // share

    def fetch(c):
        at = pl.ds(pl.multiple_of(c * HID, HID), HID)
        return pltpu.make_async_copy(w_ref.at[at], wbuf.at[c], sem.at[c])

    for c in range(chunks):
        fetch(c).start()
    last = pltpu.make_async_copy(logit_ref, lbuf, sem.at[chunks])
    last.start()
    pre_ref[...] = jnp.zeros(pre_ref.shape, F32)

    def add(c, _):
        left = jnp.concatenate([x_ref[c * per + q] for q in range(per)], axis=1)
        fetch(c).wait()
        pre_ref[...] += jnp.dot(left, wbuf[c], preferred_element_type=F32)
        return 0

    lax.fori_loop(0, chunks, add, 0)

    def squash(k, _):
        at = pl.ds(pl.multiple_of(k * PIECE, PIECE), PIECE)
        hid_ref[at] = silu(row_norm(pre_ref[at])).astype(BF16)
        return 0

    lax.fori_loop(0, rows // PIECE, squash, 0)
    last.wait()
    across = (((1,), (1,)), ((), ()))
    heads = lax.dot_general(head_ref[...], hid_ref[...], across, preferred_element_type=F32)
    pre_ref[...] = jnp.dot(hid_ref[...], lbuf[...], preferred_element_type=F32)
    spread = spread_matrix()

    def classes(k, _):
        at = pl.ds(pl.multiple_of(k * PIECE, PIECE), PIECE)
        exponent = jnp.exp(5.0 * jnp.tanh(pre_ref[at] / 5.0))
        wanted = picks_ref[at, :GROUPS]
        chosen = jnp.where(chosen_mask(wanted, spread), exponent, 0.0)
        parts_ref[0, at], parts_ref[1, at] = two_parts(exponent)
        parts_ref[2, at], parts_ref[3, at] = two_parts(chosen)
        return 0

    lax.fori_loop(0, rows // PIECE, classes, 0)

    def over_groups(k):
        return lax.dot_general(
            spread, parts_ref[k], across, preferred_element_type=F32
        ) + lax.dot_general(spread, parts_ref[k + 1], across, preferred_element_type=F32)

    chances = 0.99 * over_groups(2) / over_groups(0) + 0.01 / CLASSES
    log_prob = jnp.sum(jnp.log(chances), axis=0, keepdims=True)
    live = live_ref[:, :rows]
    out_ref[...] = jnp.zeros(out_ref.shape, F32)
    out_ref[0:1, :rows] = log_prob * live
    out_ref[1:2, :rows] = heads[0:1] * live
    out_ref[2:3, :rows] = sigmoid(heads[1:2]) * live


def pick_kernel(at_ref, own_ref, other_ref, carried_ref, low_ref, *rest_ref):
    count, per_task, share = own_ref.shape
    done = carried_ref.shape[0] // per_task
    for i in range(count):
        at = at_ref[i]
        inner = at % count
        value = jnp.where(at < count, own_ref[inner], other_ref[inner])
        low = value.astype(BF16)
        rows = slice(i * per_task, (i + 1) * per_task)
        if i < done:
            carried_ref[rows] = value
            for k in range(low_ref.shape[0]):
                low_ref[k, rows] = low
        else:
            rest_ref[0][(i - done) * per_task : (i - done + 1) * per_task] = low


def settle_kernel(at_ref, got_ref, outs_ref, to_ref, final_ref, small_ref, buf, sem):
    count, per_task, share = buf.shape
    copies = []
    for i in range(count):
        at = pl.ds(pl.multiple_of(at_ref[1, i] * per_task, per_task), per_task)
        copy = pltpu.make_async_copy(got_ref.at[at_ref[0, i], at], buf.at[i], sem.at[i])
        copy.start()
        copies.append(copy)
    parts = side_by_side(outs_ref)
    for t in range(STEPS):
        values = jnp.dot(
            parts, selector(parts.shape[1], to_ref[t : t + 1]), preferred_element_type=F32
        )
        for k in range(3):
            at = t * 3 + k
            small_ref[k, t : t + 1, :] = values[at : at + 1] + values[12 + at : 13 + at]
    for i in range(count):
        copies[i].wait()
        final_ref[i * per_task : (i + 1) * per_task] = buf[i].astype(F32)


def params(mib):
    return pltpu.CompilerParams(vmem_limit_bytes=mib * 1024 * 1024)


WHOLE = pl.BlockSpec()
STAY = pl.BlockSpec(memory_space=pltpu.HBM)
SCALARS = pl.BlockSpec(memory_space=pltpu.SMEM)


def embed(at, everyone, stoch, act, rows):
    steps, _, depth = everyone.shape
    made = pl.pallas_call(
        embed_kernel,
        in_specs=[SCALARS, WHOLE, WHOLE, WHOLE],
        out_shape=[jax.ShapeDtypeStruct((rows, HID), BF16)] * steps
        + [jax.ShapeDtypeStruct((rows, depth), BF16)] * steps,
        scratch_shapes=[
            pltpu.VMEM((rows, HID + ACT_PAD), BF16),
            pltpu.VMEM((rows, HID), F32),
        ],
        compiler_params=params(20),
        name="embed",
    )(at, everyone, stoch, act)
    return made[:steps], made[steps:]


def gates(emb, x, w):
    shards, rows, share = x.shape
    parts, depth, _ = w.shape
    return pl.pallas_call(
        gates_kernel,
        in_specs=[WHOLE, WHOLE, STAY],
        out_shape=[
            jax.ShapeDtypeStruct((rows, parts * share), F32),
            jax.ShapeDtypeStruct((shards, 2, 256), F32),
        ],
        scratch_shapes=[
            pltpu.VMEM((depth // HID, parts, HID, share), BF16),
            pltpu.SemaphoreType.DMA((depth // HID,)),
        ],
        compiler_params=params(24),
        name="gates",
    )(emb, x, w)


def renew(g, stats, carried, live, entries):
    rows, share = carried.shape
    return pl.pallas_call(
        functools.partial(update_kernel, entries),
        out_shape=[
            jax.ShapeDtypeStruct((rows, share), F32),
            jax.ShapeDtypeStruct((stats.shape[0], rows, share), BF16),
        ],
        compiler_params=params(16),
        name="renew",
    )(g, stats, carried, live)


def prior(x, w, logit, head, picks, live):
    rows = x.shape[1]
    chunks = w.shape[0] // HID
    return pl.pallas_call(
        prior_kernel,
        in_specs=[WHOLE, STAY, STAY, WHOLE, WHOLE, WHOLE],
        out_shape=jax.ShapeDtypeStruct((8, 256), F32),
        scratch_shapes=[
            pltpu.VMEM((chunks, HID, HID), BF16),
            pltpu.VMEM((HID, HID), BF16),
            pltpu.VMEM((rows, HID), F32),
            pltpu.VMEM((rows, HID), BF16),
            pltpu.VMEM((4, rows, HID), BF16),
            pltpu.SemaphoreType.DMA((chunks + 1,)),
        ],
        compiler_params=params(28),
        name="prior",
    )(x, w, logit, head, picks, live)


def pick(at, own, other, rows, shards):
    count, per_task, share = own.shape
    left = count * per_task - rows
    shapes = [
        jax.ShapeDtypeStruct((rows, share), F32),
        jax.ShapeDtypeStruct((shards, rows, share), BF16),
    ]
    if left:
        shapes.append(jax.ShapeDtypeStruct((left, share), BF16))
    return pl.pallas_call(
        pick_kernel,
        in_specs=[SCALARS, WHOLE, WHOLE],
        out_shape=shapes,
        compiler_params=params(16),
        name="pick",
    )(at, own, other)


def settle(at, got, outs, to, count, per_task):
    share = got.shape[2]
    return pl.pallas_call(
        settle_kernel,
        in_specs=[SCALARS, pl.BlockSpec(memory_space=pl.ANY), WHOLE, WHOLE],
        out_shape=[
            jax.ShapeDtypeStruct((count * per_task, share), F32),
            jax.ShapeDtypeStruct((3, STEPS, to.shape[1]), F32),
        ],
        scratch_shapes=[
            pltpu.VMEM((count, per_task, share), BF16),
            pltpu.SemaphoreType.DMA((count,)),
        ],
        compiler_params=params(16),
        name="settle",
    )(at, got, outs, to)


def exchange(copies, axis):
    return lax.all_to_all(copies, axis, 0, 0, tiled=True)


def window(count, args, holders, shards):
    (
        deter, other, draws, actions, horizons, offsets, rank, local, from_task,
        stoch, act, w, prior_weight, logit, head,
    ) = args
    all_rows, share = deter.shape
    per_core = local.shape[0]
    per_task = all_rows // per_core
    rows = count * per_task
    entries = 3 * share * shards
    place = lax.axis_index("task")
    pair = 2 * per_core
    in_block = per_core // BLK_DEV

    carried, low, *rest = pick(
        from_task,
        deter.reshape(per_core, per_task, share),
        other.reshape(per_core, per_task, share),
        rows,
        shards,
    )
    x = exchange(low, "mp")

    sent = jnp.concatenate(
        [draws, actions[:, None], jnp.zeros((STEPS, DEPTH - GROUPS - 1, all_rows), I32)], axis=1
    ).astype(BF16)
    everyone = jnp.transpose(lax.all_gather(sent, "task"), (1, 0, 3, 2))
    everyone = everyone.reshape(STEPS, holders * all_rows, DEPTH)

    task = place // 2 * pair + local
    horizon = jnp.sum(
        jnp.where(task[:, None] == jnp.arange(TASKS, dtype=I32)[None, :], horizons[None, :], 0), axis=1
    )
    moments = WSTART + jnp.arange(STEPS, dtype=I32)
    living = jnp.repeat((horizon[None, :] > moments[:, None]).astype(F32), per_task, axis=1)

    running = jnp.cumsum(offsets, axis=0) % holders
    lane_block = task % per_core // in_block
    blocks = jnp.arange(BLK_DEV, dtype=I32)
    ahead_by = jnp.sum(
        jnp.where(lane_block[None, :, None] == blocks, running[:, None, :], 0), axis=2
    )
    slot = (task[None, :] // per_core + ahead_by) % holders
    source = slot * all_rows + (task % per_core)[None, :] * per_task
    emb, picks = embed(source, everyone, stoch, act, rows)
    x, emb, picks = lax.optimization_barrier((x, emb, picks))

    held = jnp.repeat((place - running) % holders, in_block, axis=1) * per_core
    held = held + jnp.arange(per_core, dtype=I32)[None, :]
    dealt = jnp.sum(
        jnp.where(held[:, :, None] == jnp.arange(TASKS, dtype=I32), rank.reshape(-1), 0), axis=2
    )
    core = held // pair * 2 + dealt % 2
    chunk = dealt // 2
    settle_at = jnp.stack([core[STEPS - 1], chunk[STEPS - 1]])
    to = jnp.where(chunk < count, core * 256 + chunk * per_task, -TASKS * 256)
    to = jnp.repeat(to, per_task, axis=1) + jnp.arange(all_rows, dtype=I32)[None, :] % per_task

    small = []
    for moment in range(STEPS):
        live = living[moment : moment + 1]
        g, stats = gates(emb[moment], x, w)
        stats = exchange(stats, "mp")
        small.append(prior(x, prior_weight, logit, head, picks[moment], live))
        stats, small = lax.optimization_barrier((stats, small))
        carried, low = renew(g, stats, carried, live, entries)
        if moment < STEPS - 1:
            x = exchange(low, "mp")

    outs = jnp.concatenate([s[:3] for s in small], axis=0)
    high, low_part = two_parts(outs)
    sent = jnp.concatenate([low[0], *rest, high, low_part, jnp.zeros((8, share), BF16)], axis=0)
    got = exchange(jnp.broadcast_to(sent[None], (holders, *sent.shape)), "task")
    outs = got[:, all_rows : all_rows + 24]
    return settle(settle_at, got, outs, to, per_core, per_task)


def on_device(
    deter,
    draws,
    actions,
    horizons,
    offsets,
    embed_stoch,
    embed_act,
    gru_weight,
    prior_weight,
    logit_weight,
    head_weight,
):
    holders = lax.axis_size("task")
    place = lax.axis_index("task")
    shards = lax.axis_size("mp")
    rows, share = deter.shape
    per_core = TASKS // holders
    pair = 2 * per_core

    other = lax.ppermute(deter, "task", [(i, i ^ 1) for i in range(holders)])
    w = jnp.transpose(gru_weight, (1, 0, 2))
    act = jnp.pad(embed_act, ((0, ACT_PAD - embed_act.shape[0]), (0, 0)))
    head = jnp.pad(jnp.transpose(head_weight), ((0, 6), (0, 0)))

    by_chip = horizons.reshape(TASKS // pair, pair)
    index = jnp.arange(pair, dtype=I32)
    ahead = (by_chip[:, None, :] > by_chip[:, :, None]) | (
        (by_chip[:, None, :] == by_chip[:, :, None]) & (index[None, None, :] < index[None, :, None])
    )
    rank = jnp.sum(ahead.astype(I32), axis=2)
    most = jnp.max(jnp.sum((by_chip > WSTART).astype(I32), axis=1))
    need = (most + 1) // 2
    level = sum((need > n).astype(I32) for n in LEVELS[:-1])

    chip = place // 2
    mine = 2 * jnp.arange(per_core, dtype=I32) + place % 2
    my_rank = jnp.sum(
        jnp.where(jnp.arange(TASKS // pair, dtype=I32)[:, None] == chip, rank, 0), axis=0
    )
    local = jnp.sum(jnp.where(my_rank[None, :] == mine[:, None], index[None, :], 0), axis=1)
    swapped = (local // per_core != place % 2).astype(I32)
    from_task = swapped * per_core + local % per_core
    operands = (
        deter, other, draws, actions, horizons, offsets, rank, local, from_task,
        embed_stoch, act, w, prior_weight, logit_weight, head,
    )
    branches = [lambda args, n=n: window(n, args, holders, shards) for n in LEVELS]
    final, small = lax.switch(level, branches, operands)
    return (small[0], small[1], small[2], final)


def solution(mesh):
    in_specs = (
        P("task", "mp"),
        P(None, None, "task"),
        P(None, "task"),
        P(),
        P(),
        P(),
        P(),
        P(None, None, "mp"),
        P(),
        P(),
        P(),
    )
    out_specs = (P(None, "task"), P(None, "task"), P(None, "task"), P("task", "mp"))
    return jax.shard_map(
        on_device, mesh=mesh, in_specs=in_specs, out_specs=out_specs, check_vma=False
    )
```

```python
import functools

import jax
import jax.numpy as jnp
from jax import lax
from jax.experimental import pallas as pl
from jax.experimental.pallas import tpu as pltpu
from jax.sharding import PartitionSpec as P

HID = 1024
GROUPS = 32
CLASSES = 32
TASKS = 64
BLK_DEV = 4
STEPS = 4
WSTART = 16
DEPTH = 40
LEVELS = (6, 8)
PIECE = 32
ROLLED = (8,)
F32 = jnp.float32
BF16 = jnp.bfloat16
I32 = jnp.int32


def silu(v):
    return v / (1.0 + jnp.exp(-v))


def sigmoid(v):
    return 1.0 / (1.0 + jnp.exp(-v))


def row_norm(pre):
    entries = pre.shape[1]
    avg = jnp.sum(pre, axis=1, keepdims=True) / entries
    squares = jnp.sum(pre * pre, axis=1, keepdims=True) / entries
    return (pre - avg) * lax.rsqrt(squares - avg * avg + 1e-5)


def spread_matrix():
    variable = lax.broadcasted_iota(I32, (GROUPS, HID), 0)
    entry = lax.broadcasted_iota(I32, (GROUPS, HID), 1)
    return (entry // CLASSES == variable).astype(F32).astype(BF16)


def chosen_mask(by_row, spread):
    wide = jnp.dot(by_row, spread, preferred_element_type=F32)
    entry = lax.broadcasted_iota(I32, wide.shape, 1)
    return wide == (entry % CLASSES).astype(F32)


def selector(length, at):
    place = lax.broadcasted_iota(I32, (length, at.shape[1]), 0)
    return (place == at).astype(F32).astype(BF16)


def side_by_side(ref):
    return jnp.concatenate([ref[q] for q in range(ref.shape[0])], axis=1)


def embed_kernel(
    at_ref, ev_hbm, stoch_hbm, act_ref, out_hbm, hot_hbm,
    picks_ref, stoch_ref, hot_ref, out_ref, sem, done_sem,
):
    steps, rows, _ = hot_ref.shape
    count = rows // PIECE

    def fetch(step, k):
        at = pl.ds(pl.multiple_of(at_ref[step, k], PIECE), PIECE)
        to = pl.ds(k * PIECE, PIECE)
        return pltpu.make_async_copy(ev_hbm.at[step, at], picks_ref.at[step, to], sem.at[step, k])

    def give(step, q):
        ref, hbm = ((hot_ref, hot_hbm), (out_ref, out_hbm))[q]
        return pltpu.make_async_copy(ref.at[step], hbm.at[step], done_sem.at[q, step])

    def start(step, _):
        for k in range(count):
            fetch(step, k).start()
        return 0

    lax.fori_loop(0, steps, start, 0)
    table = pltpu.make_async_copy(stoch_hbm, stoch_ref, done_sem.at[2, 0])
    table.start()
    spread = spread_matrix()
    ids = lax.broadcasted_iota(I32, (rows, act_ref.shape[0]), 1).astype(F32)

    def make(step, _):
        for k in range(count):
            fetch(step, k).wait()
        wanted = picks_ref[step]
        hot = chosen_mask(wanted[:, :GROUPS], spread).astype(F32).astype(BF16)
        hot_ref[step] = hot
        give(step, 0).start()

        @pl.when(step == 0)
        def _():
            table.wait()

        action = wanted[:, GROUPS : GROUPS + 1].astype(F32)
        act_hot = (ids == action).astype(F32).astype(BF16)
        pre = jnp.dot(hot, stoch_ref[...], preferred_element_type=F32) + jnp.dot(
            act_hot, act_ref[...], preferred_element_type=F32
        )
        out_ref[step] = silu(row_norm(pre)).astype(BF16)
        give(step, 1).start()
        return 0

    lax.fori_loop(0, steps, make, 0)

    def finish(step, _):
        give(step, 0).wait()
        give(step, 1).wait()
        return 0

    lax.fori_loop(0, steps, finish, 0)


def full_lanes(part):
    rows = part.shape[0]
    if rows < 256:
        part = jnp.concatenate([part, jnp.zeros((256 - rows, 128), F32)], axis=0)
    return jnp.transpose(part)


def lanes_from_row(row, rows):
    return jnp.transpose(jnp.broadcast_to(row, (128, row.shape[1])))[:rows]


def gates_kernel(step, emb_hbm, x_ref, w_ref, g_hbm, stat_ref, g_ref, wbuf, emb_ref, sem):
    parts, depth, share = w_ref.shape
    chunks = depth // HID

    def fetch(c):
        at = pl.ds(pl.multiple_of(c * HID, HID), HID)
        return pltpu.make_async_copy(w_ref.at[:, at, :], wbuf.at[c], sem.at[c])

    emb = pltpu.make_async_copy(emb_hbm.at[step], emb_ref, sem.at[chunks])
    emb.start()
    for c in range(chunks):
        fetch(c).start()
    per = HID // share
    emb.wait()
    fetch(0).wait()
    for k in range(parts):
        g_ref[:, k * share : (k + 1) * share] = jnp.dot(
            emb_ref[...], wbuf[0, k], preferred_element_type=F32
        )

    def add(c, _):
        left = jnp.concatenate([x_ref[(c - 1) * per + q] for q in range(per)], axis=1)
        fetch(c).wait()
        for k in range(parts):
            g_ref[:, k * share : (k + 1) * share] += jnp.dot(
                left, wbuf[c, k], preferred_element_type=F32
            )
        return 0

    lax.fori_loop(1, chunks, add, 0)
    out = pltpu.make_async_copy(g_ref, g_hbm, sem.at[chunks])
    out.start()
    rows, width = g_ref.shape
    part = jnp.zeros((rows, 128), F32)
    part_sq = part
    for q in range(width // 128):
        piece = g_ref[:, q * 128 : (q + 1) * 128]
        part += piece
        part_sq += piece * piece
    sums = jnp.concatenate(
        [
            jnp.sum(full_lanes(part), axis=0, keepdims=True),
            jnp.sum(full_lanes(part_sq), axis=0, keepdims=True),
        ],
        axis=0,
    )
    for q in range(stat_ref.shape[0]):
        stat_ref[q] = sums
    out.wait()


def update_kernel(
    entries, step, g_hbm, stat_ref, carried_hbm, live_ref, new_hbm, low_ref,
    g_ref, carried_ref, new_ref, sem,
):
    copies = [
        pltpu.make_async_copy(g_hbm, g_ref, sem.at[0]),
        pltpu.make_async_copy(carried_hbm, carried_ref, sem.at[1]),
    ]
    for copy in copies:
        copy.start()
    sums = jnp.sum(stat_ref[...], axis=0) / entries
    avg = sums[0:1]
    inv = lax.rsqrt(sums[1:2] - avg * avg + 1e-5)
    rows, share = carried_ref.shape
    avg_l = lanes_from_row(avg, rows)
    inv_l = lanes_from_row(inv, rows)
    live_l = lanes_from_row(live_ref[pl.ds(step, 1), :], rows)
    for copy in copies:
        copy.wait()
    for q in range(share // 128):
        def normed(part):
            at = part * share + q * 128
            return (g_ref[:, at : at + 128] - avg_l) * inv_l

        held = carried_ref[:, q * 128 : (q + 1) * 128]
        reset = sigmoid(normed(0))
        candidate = jnp.tanh(reset * normed(1))
        update = sigmoid(normed(2) - 1.0)
        renewed = update * candidate + (1.0 - update) * held
        renewed = jnp.where(live_l > 0, renewed, held)
        new_ref[:, q * 128 : (q + 1) * 128] = renewed
        low = renewed.astype(BF16)
        for k in range(low_ref.shape[0]):
            low_ref[k, :, q * 128 : (q + 1) * 128] = low
    out = pltpu.make_async_copy(new_ref, new_hbm, sem.at[2])
    out.start()
    out.wait()


def two_parts(values):
    high = values.astype(BF16)
    return high, (values - high.astype(F32)).astype(BF16)


def prior_kernel(
    step, x_hbm, w_ref, logit_ref, head_ref, hot_hbm, live_ref, out_ref,
    x_ref, wbuf, lbuf, pre_ref, hid_ref, hot_ref, parts_ref, sem,
):
    shards, rows, share = x_ref.shape
    chunks = w_ref.shape[0] // HID
    per = HID // share

    def fetch(c):
        at = pl.ds(pl.multiple_of(c * HID, HID), HID)
        return pltpu.make_async_copy(w_ref.at[at], wbuf.at[c], sem.at[c])

    state = pltpu.make_async_copy(x_hbm, x_ref, sem.at[chunks + 2])
    state.start()
    for c in range(chunks):
        fetch(c).start()
    last = pltpu.make_async_copy(logit_ref, lbuf, sem.at[chunks])
    last.start()
    marks = pltpu.make_async_copy(hot_hbm.at[step], hot_ref, sem.at[chunks + 1])
    marks.start()
    pre_ref[...] = jnp.zeros(pre_ref.shape, F32)
    state.wait()

    def add(c, _):
        left = jnp.concatenate([x_ref[c * per + q] for q in range(per)], axis=1)
        fetch(c).wait()
        pre_ref[...] += jnp.dot(left, wbuf[c], preferred_element_type=F32)
        return 0

    lax.fori_loop(0, chunks, add, 0)

    def squash(k, _):
        at = pl.ds(pl.multiple_of(k * PIECE, PIECE), PIECE)
        hid_ref[at] = silu(row_norm(pre_ref[at])).astype(BF16)
        return 0

    lax.fori_loop(0, rows // PIECE, squash, 0)
    last.wait()
    marks.wait()
    across = (((1,), (1,)), ((), ()))
    heads = lax.dot_general(head_ref[...], hid_ref[...], across, preferred_element_type=F32)
    pre_ref[...] = jnp.dot(hid_ref[...], lbuf[...], preferred_element_type=F32)
    spread = spread_matrix()

    def classes(k, _):
        at = pl.ds(pl.multiple_of(k * PIECE, PIECE), PIECE)
        high, low = two_parts(jnp.exp(5.0 * jnp.tanh(pre_ref[at] / 5.0)))
        hot = hot_ref[at]
        parts_ref[0, at] = high
        parts_ref[1, at] = low
        parts_ref[2, at] = high * hot
        parts_ref[3, at] = low * hot
        return 0

    lax.fori_loop(0, rows // PIECE, classes, 0)

    def over_groups(k):
        return lax.dot_general(
            spread, parts_ref[k], across, preferred_element_type=F32
        ) + lax.dot_general(spread, parts_ref[k + 1], across, preferred_element_type=F32)

    chances = 0.99 * over_groups(2) / over_groups(0) + 0.01 / CLASSES
    log_prob = jnp.sum(jnp.log(chances), axis=0, keepdims=True)
    live = live_ref[pl.ds(step, 1), :rows]
    out_ref[...] = jnp.zeros(out_ref.shape, F32)
    out_ref[0:1, :rows] = log_prob * live
    out_ref[1:2, :rows] = heads[0:1] * live
    out_ref[2:3, :rows] = sigmoid(heads[1:2]) * live


def pick_kernel(at_ref, own_ref, other_ref, carried_ref, low_ref, *rest_ref):
    count, per_task, share = own_ref.shape
    done = carried_ref.shape[0] // per_task
    for i in range(count):
        at = at_ref[i]
        inner = at % count
        value = jnp.where(at < count, own_ref[inner], other_ref[inner])
        low = value.astype(BF16)
        rows = slice(i * per_task, (i + 1) * per_task)
        if i < done:
            carried_ref[rows] = value
            for k in range(low_ref.shape[0]):
                low_ref[k, rows] = low
        else:
            rest_ref[0][(i - done) * per_task : (i - done + 1) * per_task] = low


def settle_kernel(
    at_ref, got_ref, outs_ref, to_ref, log_ref, reward_ref, cont_ref, final_ref, buf, sem
):
    count, per_task, share = buf.shape
    copies = []
    for i in range(count):
        at = pl.ds(pl.multiple_of(at_ref[1, i] * per_task, per_task), per_task)
        copy = pltpu.make_async_copy(got_ref.at[at_ref[0, i], at], buf.at[i], sem.at[i])
        copy.start()
        copies.append(copy)
    parts = side_by_side(outs_ref)
    for t in range(STEPS):
        values = jnp.dot(
            parts, selector(parts.shape[1], to_ref[t : t + 1]), preferred_element_type=F32
        )
        for k, ref in enumerate((log_ref, reward_ref, cont_ref)):
            at = t * 3 + k
            ref[t : t + 1] = values[at : at + 1] + values[12 + at : 13 + at]
    for i in range(count):
        copies[i].wait()
        final_ref[i * per_task : (i + 1) * per_task] = buf[i].astype(F32)


def params(mib):
    return pltpu.CompilerParams(vmem_limit_bytes=mib * 1024 * 1024)


WHOLE = pl.BlockSpec()
STAY = pl.BlockSpec(memory_space=pltpu.HBM)
SCALARS = pl.BlockSpec(memory_space=pltpu.SMEM)


def placed(specs, operands):
    return tuple(
        pltpu.with_memory_space_constraint(o, pltpu.HBM) if s is STAY else o
        for s, o in zip(specs, operands, strict=True)
    )


def embed(at, everyone, stoch, act, rows):
    steps, _, depth = everyone.shape
    return pl.pallas_call(
        embed_kernel,
        in_specs=[SCALARS, STAY, STAY, WHOLE],
        out_specs=[STAY, STAY],
        out_shape=[pltpu.HBM((steps, rows, HID), BF16)] * 2,
        scratch_shapes=[
            pltpu.VMEM((steps, rows, depth), BF16),
            pltpu.VMEM(stoch.shape, BF16),
            pltpu.VMEM((steps, rows, HID), BF16),
            pltpu.VMEM((steps, rows, HID), BF16),
            pltpu.SemaphoreType.DMA((steps, rows // PIECE)),
            pltpu.SemaphoreType.DMA((3, steps)),
        ],
        compiler_params=params(24),
        name="embed",
    )(*placed([SCALARS, STAY, STAY, WHOLE], (at, everyone, stoch, act)))


def stepped(kernel, moment, specs, operands):
    operands = placed(specs, operands)
    if isinstance(moment, int):
        return functools.partial(kernel, moment), specs, operands

    def with_scalar(step_ref, *refs):
        kernel(step_ref[0], *refs)

    return with_scalar, [SCALARS, *specs], (jnp.full((1,), moment, I32), *operands)


def gates(moment, emb, x, w):
    kernel, specs, operands = stepped(gates_kernel, moment, [STAY, WHOLE, STAY], (emb, x, w))
    shards, rows, share = x.shape
    parts, depth, _ = w.shape
    return pl.pallas_call(
        kernel,
        in_specs=specs,
        out_shape=[
            pltpu.HBM((rows, parts * share), F32),
            jax.ShapeDtypeStruct((shards, 2, 256), F32),
        ],
        out_specs=[STAY, WHOLE],
        scratch_shapes=[
            pltpu.VMEM((rows, parts * share), F32),
            pltpu.VMEM((depth // HID, parts, HID, share), BF16),
            pltpu.VMEM((rows, HID), BF16),
            pltpu.SemaphoreType.DMA((depth // HID + 1,)),
        ],
        compiler_params=params(24),
        name="gates",
    )(*operands)


def renew(moment, g, stats, carried, live, entries):
    kernel, specs, operands = stepped(
        functools.partial(update_kernel, entries), moment, [STAY, WHOLE, STAY, WHOLE], (g, stats, carried, live)
    )
    rows, share = carried.shape
    return pl.pallas_call(
        kernel,
        in_specs=specs,
        out_shape=[
            pltpu.HBM((rows, share), F32),
            jax.ShapeDtypeStruct((stats.shape[0], rows, share), BF16),
        ],
        out_specs=[STAY, WHOLE],
        scratch_shapes=[
            pltpu.VMEM(g.shape, F32),
            pltpu.VMEM((rows, share), F32),
            pltpu.VMEM((rows, share), F32),
            pltpu.SemaphoreType.DMA((3,)),
        ],
        compiler_params=params(16),
        name="renew",
    )(*operands)


def prior(moment, x, w, logit, head, hot, live):
    kernel, specs, operands = stepped(
        prior_kernel,
        moment,
        [STAY, STAY, STAY, WHOLE, STAY, WHOLE],
        (x, w, logit, head, hot, live),
    )
    rows = x.shape[1]
    chunks = w.shape[0] // HID
    return pl.pallas_call(
        kernel,
        in_specs=specs,
        out_shape=jax.ShapeDtypeStruct((8, 256), F32),
        scratch_shapes=[
            pltpu.VMEM(x.shape, BF16),
            pltpu.VMEM((chunks, HID, HID), BF16),
            pltpu.VMEM((HID, HID), BF16),
            pltpu.VMEM((rows, HID), F32),
            pltpu.VMEM((rows, HID), BF16),
            pltpu.VMEM((rows, HID), BF16),
            pltpu.VMEM((4, rows, HID), BF16),
            pltpu.SemaphoreType.DMA((chunks + 3,)),
        ],
        compiler_params=params(28),
        name="prior",
    )(*operands)


def pick(at, own, other, rows, shards):
    count, per_task, share = own.shape
    left = count * per_task - rows
    shapes = [
        jax.ShapeDtypeStruct((rows, share), F32),
        jax.ShapeDtypeStruct((shards, rows, share), BF16),
    ]
    if left:
        shapes.append(jax.ShapeDtypeStruct((left, share), BF16))
    return pl.pallas_call(
        pick_kernel,
        in_specs=[SCALARS, WHOLE, WHOLE],
        out_shape=shapes,
        compiler_params=params(16),
        name="pick",
    )(at, own, other)


def settle(at, got, outs, to, count, per_task):
    share = got.shape[2]
    return pl.pallas_call(
        settle_kernel,
        in_specs=[SCALARS, pl.BlockSpec(memory_space=pl.ANY), WHOLE, WHOLE],
        out_shape=[jax.ShapeDtypeStruct(to.shape, F32)] * 3
        + [jax.ShapeDtypeStruct((count * per_task, share), F32)],
        scratch_shapes=[
            pltpu.VMEM((count, per_task, share), BF16),
            pltpu.SemaphoreType.DMA((count,)),
        ],
        compiler_params=params(16),
        name="settle",
    )(at, got, outs, to)


def exchange(copies, axis):
    return lax.all_to_all(copies, axis, 0, 0, tiled=True)


def window(count, args, holders, shards):
    (
        deter, other, draws, actions, horizons, offsets, rank, local, from_task,
        stoch, act, w, prior_weight, logit, head,
    ) = args
    all_rows, share = deter.shape
    per_core = local.shape[0]
    per_task = all_rows // per_core
    rows = count * per_task
    entries = 3 * share * shards
    place = lax.axis_index("task")
    pair = 2 * per_core
    in_block = per_core // BLK_DEV

    carried, low, *rest = pick(
        from_task,
        deter.reshape(per_core, per_task, share),
        other.reshape(per_core, per_task, share),
        rows,
        shards,
    )
    x = exchange(low, "mp")

    sent = jnp.concatenate(
        [draws, actions[:, None], jnp.zeros((STEPS, DEPTH - GROUPS - 1, all_rows), I32)], axis=1
    ).astype(BF16)
    everyone = jnp.transpose(lax.all_gather(sent, "task"), (1, 0, 3, 2))
    everyone = everyone.reshape(STEPS, holders * all_rows, DEPTH)

    task = place // 2 * pair + local
    horizon = jnp.sum(
        jnp.where(task[:, None] == jnp.arange(TASKS, dtype=I32)[None, :], horizons[None, :], 0), axis=1
    )
    moments = WSTART + jnp.arange(STEPS, dtype=I32)
    living = jnp.repeat((horizon[None, :] > moments[:, None]).astype(F32), per_task, axis=1)

    running = jnp.cumsum(offsets, axis=0) % holders
    lane_block = task % per_core // in_block
    blocks = jnp.arange(BLK_DEV, dtype=I32)
    ahead_by = jnp.sum(
        jnp.where(lane_block[None, :, None] == blocks, running[:, None, :], 0), axis=2
    )
    slot = (task[None, :] // per_core + ahead_by) % holders
    source = slot * all_rows + (task % per_core)[None, :] * per_task
    emb, hot = embed(source, everyone, stoch, act, rows)
    x, emb, hot = lax.optimization_barrier((x, emb, hot))

    held = jnp.repeat((place - running) % holders, in_block, axis=1) * per_core
    held = held + jnp.arange(per_core, dtype=I32)[None, :]
    dealt = jnp.sum(
        jnp.where(held[:, :, None] == jnp.arange(TASKS, dtype=I32), rank.reshape(-1), 0), axis=2
    )
    core = held // pair * 2 + dealt % 2
    chunk = dealt // 2
    settle_at = jnp.stack([core[STEPS - 1], chunk[STEPS - 1]])
    to = jnp.where(chunk < count, core * 256 + chunk * per_task, -TASKS * 256)
    to = jnp.repeat(to, per_task, axis=1) + jnp.arange(all_rows, dtype=I32)[None, :] % per_task

    def one_step(moment, x, carried):
        g, stats = gates(moment, emb, x, w)
        stats = exchange(stats, "mp")
        small = prior(moment, x, prior_weight, logit, head, hot, living)
        stats, small = lax.optimization_barrier((stats, small))
        carried, low = renew(moment, g, stats, carried, living, entries)
        return low, carried, small[:3]

    small = []
    if count in ROLLED:

        def body(state, moment):
            low, carried, out = one_step(moment, *state)
            return (exchange(low, "mp"), carried), out

        (x, carried), outs = lax.scan(body, (x, carried), jnp.arange(STEPS - 1, dtype=I32))
        small.append(outs.reshape(-1, outs.shape[2]))
    else:
        for moment in range(STEPS - 1):
            low, carried, out = one_step(moment, x, carried)
            small.append(out)
            x = exchange(low, "mp")
    low, _, out = one_step(STEPS - 1, x, carried)

    outs = jnp.concatenate([*small, out], axis=0)
    high, low_part = two_parts(outs)
    sent = jnp.concatenate([low[0], *rest, high, low_part, jnp.zeros((8, share), BF16)], axis=0)
    got = exchange(jnp.broadcast_to(sent[None], (holders, *sent.shape)), "task")
    outs = got[:, all_rows : all_rows + 24]
    return settle(settle_at, got, outs, to, per_core, per_task)


def on_device(
    deter,
    draws,
    actions,
    horizons,
    offsets,
    embed_stoch,
    embed_act,
    gru_weight,
    prior_weight,
    logit_weight,
    head_weight,
):
    holders = lax.axis_size("task")
    place = lax.axis_index("task")
    shards = lax.axis_size("mp")
    rows, share = deter.shape
    per_core = TASKS // holders
    pair = 2 * per_core

    other = lax.ppermute(deter, "task", [(i, i ^ 1) for i in range(holders)])
    w = jnp.transpose(gru_weight, (1, 0, 2))
    head = jnp.transpose(head_weight)

    by_chip = horizons.reshape(TASKS // pair, pair)
    index = jnp.arange(pair, dtype=I32)
    ahead = (by_chip[:, None, :] > by_chip[:, :, None]) | (
        (by_chip[:, None, :] == by_chip[:, :, None]) & (index[None, None, :] < index[None, :, None])
    )
    rank = jnp.sum(ahead.astype(I32), axis=2)
    most = jnp.max(jnp.sum((by_chip > WSTART).astype(I32), axis=1))
    need = (most + 1) // 2
    level = sum((need > n).astype(I32) for n in LEVELS[:-1])

    chip = place // 2
    mine = 2 * jnp.arange(per_core, dtype=I32) + place % 2
    my_rank = jnp.sum(
        jnp.where(jnp.arange(TASKS // pair, dtype=I32)[:, None] == chip, rank, 0), axis=0
    )
    local = jnp.sum(jnp.where(my_rank[None, :] == mine[:, None], index[None, :], 0), axis=1)
    swapped = (local // per_core != place % 2).astype(I32)
    from_task = swapped * per_core + local % per_core
    operands = (
        deter, other, draws, actions, horizons, offsets, rank, local, from_task,
        embed_stoch, embed_act, w, prior_weight, logit_weight, head,
    )
    branches = [lambda args, n=n: window(n, args, holders, shards) for n in LEVELS]
    return tuple(lax.switch(level, branches, operands))


def solution(mesh):
    in_specs = (
        P("task", "mp"),
        P(None, None, "task"),
        P(None, "task"),
        P(),
        P(),
        P(),
        P(),
        P(None, None, "mp"),
        P(),
        P(),
        P(),
    )
    out_specs = (P(None, "task"), P(None, "task"), P(None, "task"), P("task", "mp"))
    return jax.shard_map(
        on_device, mesh=mesh, in_specs=in_specs, out_specs=out_specs, check_vma=False
    )
```

```python
import functools

import jax
import jax.numpy as jnp
from jax import lax
from jax.experimental import pallas as pl
from jax.experimental.pallas import tpu as pltpu
from jax.sharding import PartitionSpec as P

HID = 1024
GROUPS = 32
CLASSES = 32
TASKS = 64
BLK_DEV = 4
STEPS = 4
WSTART = 16
DEPTH = 40
LEVELS = (6, 8)
PIECE = 32
ROLLED = (8,)
F32 = jnp.float32
BF16 = jnp.bfloat16
I32 = jnp.int32


def silu(v):
    return v * sigmoid(v)


def sigmoid(v):
    return 0.5 + 0.5 * jnp.tanh(0.5 * v)


def row_norm(pre):
    entries = pre.shape[1]
    avg = jnp.sum(pre, axis=1, keepdims=True) / entries
    squares = jnp.sum(pre * pre, axis=1, keepdims=True) / entries
    return (pre - avg) * lax.rsqrt(squares - avg * avg + 1e-5)


def spread_matrix():
    variable = lax.broadcasted_iota(I32, (GROUPS, HID), 0)
    entry = lax.broadcasted_iota(I32, (GROUPS, HID), 1)
    return (entry // CLASSES == variable).astype(F32).astype(BF16)


def chosen_mask(by_row, spread):
    wide = jnp.dot(by_row, spread, preferred_element_type=F32)
    entry = lax.broadcasted_iota(I32, wide.shape, 1)
    return wide == (entry % CLASSES).astype(F32)


def selector(length, at):
    place = lax.broadcasted_iota(I32, (length, at.shape[1]), 0)
    return (place == at).astype(F32).astype(BF16)


def side_by_side(ref):
    return jnp.concatenate([ref[q] for q in range(ref.shape[0])], axis=1)


def embed_kernel(
    first, at_ref, ev_hbm, stoch_hbm, act_ref, out_hbm, hot_hbm,
    picks_ref, stoch_ref, hot_ref, out_ref, sem, done_sem,
):
    steps, rows, _ = hot_ref.shape
    count = rows // PIECE

    def fetch(step, k):
        at = pl.ds(pl.multiple_of(at_ref[first + step, k], PIECE), PIECE)
        to = pl.ds(k * PIECE, PIECE)
        return pltpu.make_async_copy(
            ev_hbm.at[first + step, at], picks_ref.at[step, to], sem.at[step, k]
        )

    def give(step, q):
        ref, hbm = ((hot_ref, hot_hbm), (out_ref, out_hbm))[q]
        return pltpu.make_async_copy(ref.at[step], hbm.at[step], done_sem.at[q, step])

    def start(step, _):
        for k in range(count):
            fetch(step, k).start()
        return 0

    lax.fori_loop(0, steps, start, 0)
    table = pltpu.make_async_copy(stoch_hbm, stoch_ref, done_sem.at[2, 0])
    table.start()
    spread = spread_matrix()
    ids = lax.broadcasted_iota(I32, (rows, act_ref.shape[0]), 1).astype(F32)

    def make(step, _):
        for k in range(count):
            fetch(step, k).wait()
        wanted = picks_ref[step]
        hot = chosen_mask(wanted[:, :GROUPS], spread).astype(F32).astype(BF16)
        hot_ref[step] = hot
        give(step, 0).start()

        @pl.when(step == 0)
        def _():
            table.wait()

        action = wanted[:, GROUPS : GROUPS + 1].astype(F32)
        act_hot = (ids == action).astype(F32).astype(BF16)
        pre = jnp.dot(hot, stoch_ref[...], preferred_element_type=F32) + jnp.dot(
            act_hot, act_ref[...], preferred_element_type=F32
        )
        out_ref[step] = silu(row_norm(pre)).astype(BF16)
        give(step, 1).start()
        return 0

    lax.fori_loop(0, steps, make, 0)

    def finish(step, _):
        give(step, 0).wait()
        give(step, 1).wait()
        return 0

    lax.fori_loop(0, steps, finish, 0)


def full_lanes(part):
    rows = part.shape[0]
    if rows < 256:
        part = jnp.concatenate([part, jnp.zeros((256 - rows, 128), F32)], axis=0)
    return jnp.transpose(part)


def lanes_from_row(row, rows):
    return jnp.transpose(jnp.broadcast_to(row, (128, row.shape[1])))[:rows]


def gates_kernel(step, emb_hbm, x_hbm, w_ref, g_ref, stat_ref, x_ref, wbuf, emb_ref, sem):
    parts, depth, share = w_ref.shape
    chunks = depth // HID

    def fetch(c):
        at = pl.ds(pl.multiple_of(c * HID, HID), HID)
        return pltpu.make_async_copy(w_ref.at[:, at, :], wbuf.at[c], sem.at[c])

    emb = pltpu.make_async_copy(emb_hbm.at[step], emb_ref, sem.at[chunks])
    per = HID // share

    def fetch_x(c):
        at = pl.ds((c - 1) * per, per)
        return pltpu.make_async_copy(x_hbm.at[at], x_ref.at[at], sem.at[chunks + c])

    emb.start()
    fetch(0).start()
    for c in range(1, chunks):
        fetch_x(c).start()
        fetch(c).start()
    emb.wait()
    fetch(0).wait()
    for k in range(parts):
        g_ref[:, k * share : (k + 1) * share] = jnp.dot(
            emb_ref[...], wbuf[0, k], preferred_element_type=F32
        )

    def add(c, _):
        fetch_x(c).wait()
        left = jnp.concatenate([x_ref[(c - 1) * per + q] for q in range(per)], axis=1)
        fetch(c).wait()
        for k in range(parts):
            g_ref[:, k * share : (k + 1) * share] += jnp.dot(
                left, wbuf[c, k], preferred_element_type=F32
            )
        return 0

    lax.fori_loop(1, chunks, add, 0)
    rows, width = g_ref.shape
    part = jnp.zeros((rows, 128), F32)
    part_sq = part
    for q in range(width // 128):
        piece = g_ref[:, q * 128 : (q + 1) * 128]
        part += piece
        part_sq += piece * piece
    sums = jnp.concatenate(
        [
            jnp.sum(full_lanes(part), axis=0, keepdims=True),
            jnp.sum(full_lanes(part_sq), axis=0, keepdims=True),
        ],
        axis=0,
    )
    for q in range(stat_ref.shape[0]):
        stat_ref[q] = sums


def update_kernel(entries, step, g_ref, stat_ref, carried_ref, live_ref, new_ref, low_ref):
    sums = jnp.sum(stat_ref[...], axis=0) / entries
    avg = sums[0:1]
    inv = lax.rsqrt(sums[1:2] - avg * avg + 1e-5)
    rows, share = carried_ref.shape
    avg_l = lanes_from_row(avg, rows)
    inv_l = lanes_from_row(inv, rows)
    live_l = lanes_from_row(live_ref[pl.ds(step, 1), :], rows)
    for q in range(share // 128):
        def normed(part):
            at = part * share + q * 128
            return (g_ref[:, at : at + 128] - avg_l) * inv_l

        held = carried_ref[:, q * 128 : (q + 1) * 128]
        reset = sigmoid(normed(0))
        candidate = jnp.tanh(reset * normed(1))
        update = sigmoid(normed(2) - 1.0)
        renewed = update * candidate + (1.0 - update) * held
        renewed = jnp.where(live_l > 0, renewed, held)
        new_ref[:, q * 128 : (q + 1) * 128] = renewed
        low = renewed.astype(BF16)
        for k in range(low_ref.shape[0]):
            low_ref[k, :, q * 128 : (q + 1) * 128] = low


def two_parts(values):
    high = values.astype(BF16)
    return high, (values - high.astype(F32)).astype(BF16)


def prior_kernel(
    at_step, step, x_hbm, w_ref, logit_ref, head_ref, hot_hbm, live_ref, out_ref,
    x_ref, wbuf, lbuf, pre_ref, hid_ref, hot_ref, parts_ref, sem,
):
    shards, rows, share = x_ref.shape
    chunks = w_ref.shape[0] // HID
    per = HID // share

    def fetch(c):
        at = pl.ds(pl.multiple_of(c * HID, HID), HID)
        return pltpu.make_async_copy(w_ref.at[at], wbuf.at[c], sem.at[c])

    state = pltpu.make_async_copy(x_hbm, x_ref, sem.at[chunks + 2])
    state.start()
    for c in range(chunks):
        fetch(c).start()
    last = pltpu.make_async_copy(logit_ref, lbuf, sem.at[chunks])
    last.start()
    marks = pltpu.make_async_copy(hot_hbm.at[at_step], hot_ref, sem.at[chunks + 1])
    marks.start()
    pre_ref[...] = jnp.zeros(pre_ref.shape, F32)
    state.wait()

    def add(c, _):
        left = jnp.concatenate([x_ref[c * per + q] for q in range(per)], axis=1)
        fetch(c).wait()
        pre_ref[...] += jnp.dot(left, wbuf[c], preferred_element_type=F32)
        return 0

    lax.fori_loop(0, chunks, add, 0)

    def squash(k, _):
        at = pl.ds(pl.multiple_of(k * PIECE, PIECE), PIECE)
        hid_ref[at] = silu(row_norm(pre_ref[at])).astype(BF16)
        return 0

    lax.fori_loop(0, rows // PIECE, squash, 0)
    last.wait()
    marks.wait()
    across = (((1,), (1,)), ((), ()))
    heads = lax.dot_general(head_ref[...], hid_ref[...], across, preferred_element_type=F32)
    pre_ref[...] = jnp.dot(hid_ref[...], lbuf[...], preferred_element_type=F32)
    spread = spread_matrix()

    def classes(k, _):
        at = pl.ds(pl.multiple_of(k * PIECE, PIECE), PIECE)
        high, low = two_parts(jnp.exp(5.0 * jnp.tanh(pre_ref[at] / 5.0)))
        hot = hot_ref[at]
        parts_ref[0, at] = high
        parts_ref[1, at] = low
        parts_ref[2, at] = high * hot
        parts_ref[3, at] = low * hot
        return 0

    lax.fori_loop(0, rows // PIECE, classes, 0)

    def over_groups(k):
        return lax.dot_general(
            spread, parts_ref[k], across, preferred_element_type=F32
        ) + lax.dot_general(spread, parts_ref[k + 1], across, preferred_element_type=F32)

    chances = 0.99 * over_groups(2) / over_groups(0) + 0.01 / CLASSES
    log_prob = jnp.sum(jnp.log(chances), axis=0, keepdims=True)
    live = live_ref[pl.ds(step, 1), :rows]
    out_ref[...] = jnp.zeros(out_ref.shape, F32)
    out_ref[0:1, :rows] = log_prob * live
    out_ref[1:2, :rows] = heads[0:1] * live
    out_ref[2:3, :rows] = sigmoid(heads[1:2]) * live


def pick_kernel(at_ref, own_ref, other_ref, carried_ref, low_ref, *rest_ref):
    count, per_task, share = own_ref.shape
    done = carried_ref.shape[0] // per_task
    for i in range(count):
        at = at_ref[i]
        inner = at % count
        value = jnp.where(at < count, own_ref[inner], other_ref[inner])
        low = value.astype(BF16)
        rows = slice(i * per_task, (i + 1) * per_task)
        if i < done:
            carried_ref[rows] = value
            for k in range(low_ref.shape[0]):
                low_ref[k, rows] = low
        else:
            rest_ref[0][(i - done) * per_task : (i - done + 1) * per_task] = low


def settle_kernel(
    rows, at_ref, got_ref, left_ref, outs_ref, to_ref, log_ref, reward_ref, cont_ref, final_ref, buf, sem
):
    count, per_task, share = buf.shape
    done = rows // per_task
    for i in range(count):
        chunk = at_ref[1, i]

        def bring(ref, chunk, i=i):
            at = pl.ds(pl.multiple_of(chunk * per_task, per_task), per_task)
            pltpu.make_async_copy(ref.at[at_ref[0, i], at], buf.at[i], sem.at[i]).start()

        if done == count:
            bring(got_ref, chunk)
        else:
            pl.when(chunk < done)(functools.partial(bring, got_ref, chunk))
            pl.when(chunk >= done)(functools.partial(bring, left_ref, chunk - done))
    parts = side_by_side(outs_ref)
    for t in range(STEPS):
        values = jnp.dot(
            parts, selector(parts.shape[1], to_ref[t : t + 1]), preferred_element_type=F32
        )
        for k, ref in enumerate((log_ref, reward_ref, cont_ref)):
            at = t * 3 + k
            ref[t : t + 1] = values[at : at + 1] + values[12 + at : 13 + at]
    for i in range(count):
        pltpu.make_async_copy(got_ref.at[0, pl.ds(0, per_task)], buf.at[i], sem.at[i]).wait()
        final_ref[i * per_task : (i + 1) * per_task] = buf[i].astype(F32)


def params(mib):
    return pltpu.CompilerParams(vmem_limit_bytes=mib * 1024 * 1024)


WHOLE = pl.BlockSpec()
STAY = pl.BlockSpec(memory_space=pltpu.HBM)
EITHER = pl.BlockSpec(memory_space=pl.ANY)
SCALARS = pl.BlockSpec(memory_space=pltpu.SMEM)


def placed(specs, operands):
    return tuple(
        pltpu.with_memory_space_constraint(o, pltpu.HBM) if s is STAY else o
        for s, o in zip(specs, operands, strict=True)
    )


def embed(first, steps, at, everyone, stoch, act, rows):
    depth = everyone.shape[2]
    return pl.pallas_call(
        functools.partial(embed_kernel, first),
        in_specs=[SCALARS, STAY, STAY, WHOLE],
        out_specs=[STAY, STAY],
        out_shape=[pltpu.HBM((steps, rows, HID), BF16)] * 2,
        scratch_shapes=[
            pltpu.VMEM((steps, rows, depth), BF16),
            pltpu.VMEM(stoch.shape, BF16),
            pltpu.VMEM((steps, rows, HID), BF16),
            pltpu.VMEM((steps, rows, HID), BF16),
            pltpu.SemaphoreType.DMA((steps, rows // PIECE)),
            pltpu.SemaphoreType.DMA((3, steps)),
        ],
        compiler_params=params(24),
        name="embed",
    )(*placed([SCALARS, STAY, STAY, WHOLE], (at, everyone, stoch, act)))


def stepped(kernel, steps, specs, operands):
    operands = placed(specs, operands)
    if all(isinstance(step, int) for step in steps):
        return functools.partial(kernel, *steps), specs, operands

    def with_scalars(step_ref, *refs):
        kernel(*(step_ref[k] for k in range(len(steps))), *refs)

    return with_scalars, [SCALARS, *specs], (jnp.stack(steps), *operands)


def gates(at, emb, x, w):
    kernel, specs, operands = stepped(gates_kernel, (at,), [STAY, EITHER, STAY], (emb, x, w))
    shards, rows, share = x.shape
    parts, depth, _ = w.shape
    return pl.pallas_call(
        kernel,
        in_specs=specs,
        out_shape=[
            jax.ShapeDtypeStruct((rows, parts * share), F32),
            jax.ShapeDtypeStruct((shards, 2, 256), F32),
        ],
        scratch_shapes=[
            pltpu.VMEM(x.shape, BF16),
            pltpu.VMEM((depth // HID, parts, HID, share), BF16),
            pltpu.VMEM((rows, HID), BF16),
            pltpu.SemaphoreType.DMA((2 * (depth // HID),)),
        ],
        compiler_params=params(24),
        name="gates",
    )(*operands)


def renew(moment, g, stats, carried, live, entries):
    kernel, specs, operands = stepped(
        functools.partial(update_kernel, entries), (moment,), [WHOLE] * 4, (g, stats, carried, live)
    )
    rows, share = carried.shape
    return pl.pallas_call(
        kernel,
        in_specs=specs,
        out_shape=[
            jax.ShapeDtypeStruct((rows, share), F32),
            jax.ShapeDtypeStruct((stats.shape[0], rows, share), BF16),
        ],
        compiler_params=params(16),
        name="renew",
    )(*operands)


def prior(at, moment, x, w, logit, head, hot, live):
    kernel, specs, operands = stepped(
        prior_kernel,
        (at, moment),
        [STAY, STAY, STAY, WHOLE, STAY, WHOLE],
        (x, w, logit, head, hot, live),
    )
    rows = x.shape[1]
    chunks = w.shape[0] // HID
    return pl.pallas_call(
        kernel,
        in_specs=specs,
        out_shape=jax.ShapeDtypeStruct((8, 256), F32),
        scratch_shapes=[
            pltpu.VMEM(x.shape, BF16),
            pltpu.VMEM((chunks, HID, HID), BF16),
            pltpu.VMEM((HID, HID), BF16),
            pltpu.VMEM((rows, HID), F32),
            pltpu.VMEM((rows, HID), BF16),
            pltpu.VMEM((rows, HID), BF16),
            pltpu.VMEM((4, rows, HID), BF16),
            pltpu.SemaphoreType.DMA((chunks + 3,)),
        ],
        compiler_params=params(28),
        name="prior",
    )(*operands)


def pick(at, own, other, rows, shards):
    count, per_task, share = own.shape
    left = count * per_task - rows
    shapes = [
        jax.ShapeDtypeStruct((rows, share), F32),
        jax.ShapeDtypeStruct((shards, rows, share), BF16),
    ]
    if left:
        shapes.append(jax.ShapeDtypeStruct((left, share), BF16))
    return pl.pallas_call(
        pick_kernel,
        in_specs=[SCALARS, WHOLE, WHOLE],
        out_shape=shapes,
        compiler_params=params(16),
        name="pick",
    )(at, own, other)


def settle(at, got, left, outs, to, rows, count, per_task):
    share = got.shape[2]
    return pl.pallas_call(
        functools.partial(settle_kernel, rows),
        in_specs=[SCALARS, EITHER, EITHER, WHOLE, WHOLE],
        out_shape=[jax.ShapeDtypeStruct(to.shape, F32)] * 3
        + [jax.ShapeDtypeStruct((count * per_task, share), F32)],
        scratch_shapes=[
            pltpu.VMEM((count, per_task, share), BF16),
            pltpu.SemaphoreType.DMA((count,)),
        ],
        compiler_params=params(16),
        name="settle",
    )(at, got, left, outs, to)


def exchange(copies, axis):
    return lax.all_to_all(copies, axis, 0, 0, tiled=True)


def window(count, args, holders, shards):
    (
        deter, other, draws, actions, horizons, offsets, rank, local, from_task,
        stoch, act, w, prior_weight, logit, head,
    ) = args
    all_rows, share = deter.shape
    per_core = local.shape[0]
    per_task = all_rows // per_core
    rows = count * per_task
    entries = 3 * share * shards
    place = lax.axis_index("task")
    pair = 2 * per_core
    in_block = per_core // BLK_DEV

    carried, low, *rest = pick(
        from_task,
        deter.reshape(per_core, per_task, share),
        other.reshape(per_core, per_task, share),
        rows,
        shards,
    )
    x = exchange(low, "mp")

    sent = jnp.concatenate(
        [draws, actions[:, None], jnp.zeros((STEPS, DEPTH - GROUPS - 1, all_rows), I32)], axis=1
    ).astype(BF16)
    sent = jnp.concatenate([sent.reshape(STEPS * DEPTH, all_rows), *rest], axis=0)
    everyone = lax.all_gather(sent, "task")
    left = everyone[:, STEPS * DEPTH :]
    everyone = everyone[:, : STEPS * DEPTH].reshape(holders, STEPS, DEPTH, all_rows)
    everyone = jnp.transpose(everyone, (1, 0, 3, 2)).reshape(STEPS, holders * all_rows, DEPTH)

    task = place // 2 * pair + local
    horizon = jnp.sum(
        jnp.where(task[:, None] == jnp.arange(TASKS, dtype=I32)[None, :], horizons[None, :], 0), axis=1
    )
    moments = WSTART + jnp.arange(STEPS, dtype=I32)
    living = jnp.repeat((horizon[None, :] > moments[:, None]).astype(F32), per_task, axis=1)

    running = jnp.cumsum(offsets, axis=0) % holders
    lane_block = task % per_core // in_block
    blocks = jnp.arange(BLK_DEV, dtype=I32)
    ahead_by = jnp.sum(
        jnp.where(lane_block[None, :, None] == blocks, running[:, None, :], 0), axis=2
    )
    slot = (task[None, :] // per_core + ahead_by) % holders
    source = slot * all_rows + (task % per_core)[None, :] * per_task
    first = STEPS if count in ROLLED else 1
    emb, hot = embed(0, first, source, everyone, stoch, act, rows)
    x, emb, hot = lax.optimization_barrier((x, emb, hot))

    held = jnp.repeat((place - running) % holders, in_block, axis=1) * per_core
    held = held + jnp.arange(per_core, dtype=I32)[None, :]
    dealt = jnp.sum(
        jnp.where(held[:, :, None] == jnp.arange(TASKS, dtype=I32), rank.reshape(-1), 0), axis=2
    )
    core = held // pair * 2 + dealt % 2
    chunk = dealt // 2
    settle_at = jnp.stack([core[STEPS - 1], chunk[STEPS - 1]])
    to = jnp.where(chunk < count, core * 256 + chunk * per_task, -TASKS * 256)
    to = jnp.repeat(to, per_task, axis=1) + jnp.arange(all_rows, dtype=I32)[None, :] % per_task

    def likely(at, moment, x, hot):
        return prior(at, moment, x, prior_weight, logit, head, hot, living)[:3]

    def gated(at, moment, x, emb, carried):
        g, stats = gates(at, emb, x, w)
        stats = exchange(stats, "mp")
        return renew(moment, g, stats, carried, living, entries)

    small = []
    if count in ROLLED:

        def body(state, moment):
            x, carried = state
            carried, low = gated(moment, moment, x, emb, carried)
            out = likely(moment, moment, x, hot)
            x, out = lax.optimization_barrier((exchange(low, "mp"), out))
            return (x, carried), out

        (x, carried), outs = lax.scan(body, (x, carried), jnp.arange(STEPS - 1, dtype=I32))
        small.append(outs.reshape(-1, outs.shape[2]))
        at = STEPS - 1
    else:
        at = 0
        for moment in range(STEPS - 1):
            carried, low = gated(at, moment, x, emb, carried)
            out = likely(at, moment, x, hot)
            if moment == 0:
                emb, hot = embed(1, STEPS - 1, source, everyone, stoch, act, rows)
            x = exchange(low, "mp")
            x, out, emb, hot = lax.optimization_barrier((x, out, emb, hot))
            small.append(out)
            at = moment

    g, stats = gates(at, emb, x, w)
    stats = exchange(stats, "mp")
    out = likely(at, STEPS - 1, x, hot)
    stats, small, out = lax.optimization_barrier((stats, small, out))
    _, low = renew(STEPS - 1, g, stats, carried, living, entries)

    outs = jnp.concatenate([*small, out], axis=0)
    high, low_part = two_parts(outs)
    sent = jnp.concatenate([low[0], high, low_part, jnp.zeros((8, share), BF16)], axis=0)
    got = exchange(jnp.broadcast_to(sent[None], (holders, *sent.shape)), "task")
    outs = got[:, rows : rows + 24]
    if not rest:
        left = got
    return settle(settle_at, got, left, outs, to, rows, per_core, per_task)


def on_device(
    deter,
    draws,
    actions,
    horizons,
    offsets,
    embed_stoch,
    embed_act,
    gru_weight,
    prior_weight,
    logit_weight,
    head_weight,
):
    holders = lax.axis_size("task")
    place = lax.axis_index("task")
    shards = lax.axis_size("mp")
    rows, share = deter.shape
    per_core = TASKS // holders
    pair = 2 * per_core

    other = lax.ppermute(deter, "task", [(i, i ^ 1) for i in range(holders)])
    w = jnp.transpose(gru_weight, (1, 0, 2))
    head = jnp.transpose(head_weight)

    by_chip = horizons.reshape(TASKS // pair, pair)
    index = jnp.arange(pair, dtype=I32)
    ahead = (by_chip[:, None, :] > by_chip[:, :, None]) | (
        (by_chip[:, None, :] == by_chip[:, :, None]) & (index[None, None, :] < index[None, :, None])
    )
    rank = jnp.sum(ahead.astype(I32), axis=2)
    most = jnp.max(jnp.sum((by_chip > WSTART).astype(I32), axis=1))
    need = (most + 1) // 2
    level = sum((need > n).astype(I32) for n in LEVELS[:-1])

    chip = place // 2
    mine = 2 * jnp.arange(per_core, dtype=I32) + place % 2
    my_rank = jnp.sum(
        jnp.where(jnp.arange(TASKS // pair, dtype=I32)[:, None] == chip, rank, 0), axis=0
    )
    local = jnp.sum(jnp.where(my_rank[None, :] == mine[:, None], index[None, :], 0), axis=1)
    swapped = (local // per_core != place % 2).astype(I32)
    from_task = swapped * per_core + local % per_core
    operands = (
        deter, other, draws, actions, horizons, offsets, rank, local, from_task,
        embed_stoch, embed_act, w, prior_weight, logit_weight, head,
    )
    branches = [lambda args, n=n: window(n, args, holders, shards) for n in LEVELS]
    return tuple(lax.switch(level, branches, operands))


def solution(mesh):
    in_specs = (
        P("task", "mp"),
        P(None, None, "task"),
        P(None, "task"),
        P(),
        P(),
        P(),
        P(),
        P(None, None, "mp"),
        P(),
        P(),
        P(),
    )
    out_specs = (P(None, "task"), P(None, "task"), P(None, "task"), P("task", "mp"))
    return jax.shard_map(
        on_device, mesh=mesh, in_specs=in_specs, out_specs=out_specs, check_vma=False
    )
```

```python
import functools

import jax
import jax.numpy as jnp
from jax import lax
from jax.experimental import pallas as pl
from jax.experimental.pallas import tpu as pltpu
from jax.sharding import PartitionSpec as P

HID = 1024
GROUPS = 32
CLASSES = 32
TASKS = 64
BLK_DEV = 4
STEPS = 4
WSTART = 16
DEPTH = GROUPS + 1
LEVELS = (6, 8)
PIECE = 32
ROLLED = (8,)
F32 = jnp.float32
BF16 = jnp.bfloat16
I32 = jnp.int32


def silu(v):
    return v * sigmoid(v)


def sigmoid(v):
    return 0.5 + 0.5 * jnp.tanh(0.5 * v)


def row_norm(pre):
    entries = pre.shape[1]
    avg = jnp.sum(pre, axis=1, keepdims=True) / entries
    squares = jnp.sum(pre * pre, axis=1, keepdims=True) / entries
    return (pre - avg) * lax.rsqrt(squares - avg * avg + 1e-5)


def spread_matrix():
    variable = lax.broadcasted_iota(I32, (GROUPS, HID), 0)
    entry = lax.broadcasted_iota(I32, (GROUPS, HID), 1)
    return (entry // CLASSES == variable).astype(F32).astype(BF16)


def chosen_mask(by_row, spread):
    wide = jnp.dot(by_row, spread, preferred_element_type=F32)
    entry = lax.broadcasted_iota(I32, wide.shape, 1)
    return wide == (entry % CLASSES).astype(F32)


def embed_kernel(
    first, at_ref, ev_hbm, stoch_hbm, act_ref, w_hbm, out_hbm, hot_hbm,
    picks_ref, stoch_ref, wbuf, hot_ref, out_ref, sem, done_sem,
):
    steps, rows, _ = hot_ref.shape
    count = rows // PIECE

    def fetch(step, k):
        at = pl.ds(pl.multiple_of(at_ref[first + step, k], PIECE), PIECE)
        to = pl.ds(k * PIECE, PIECE)
        return pltpu.make_async_copy(
            ev_hbm.at[first + step, at], picks_ref.at[step, to], sem.at[step, k]
        )

    def give(step, q):
        ref, hbm = ((hot_ref, hot_hbm), (out_ref, out_hbm))[q]
        return pltpu.make_async_copy(ref.at[step], hbm.at[step], done_sem.at[q, step])

    def start(step, _):
        for k in range(count):
            fetch(step, k).start()
        return 0

    lax.fori_loop(0, steps, start, 0)
    table = pltpu.make_async_copy(stoch_hbm, stoch_ref, done_sem.at[2, 0])
    table.start()
    weights = pltpu.make_async_copy(w_hbm.at[:, pl.ds(0, HID), :], wbuf, done_sem.at[2, 1])
    weights.start()
    spread = spread_matrix()
    ids = lax.broadcasted_iota(I32, (rows, act_ref.shape[0]), 1).astype(F32)

    def make(step, _):
        for k in range(count):
            fetch(step, k).wait()
        wanted = picks_ref[step]
        hot = chosen_mask(wanted[:, :GROUPS], spread).astype(F32).astype(BF16)
        hot_ref[step] = hot
        give(step, 0).start()

        @pl.when(step == 0)
        def _():
            table.wait()

        action = wanted[:, GROUPS : GROUPS + 1].astype(F32)
        act_hot = (ids == action).astype(F32).astype(BF16)
        pre = jnp.dot(hot, stoch_ref[...], preferred_element_type=F32) + jnp.dot(
            act_hot, act_ref[...], preferred_element_type=F32
        )
        embedded = silu(row_norm(pre)).astype(BF16)

        @pl.when(step == 0)
        def _():
            weights.wait()

        share = wbuf.shape[2]
        for k in range(wbuf.shape[0]):
            out_ref[step, :, k * share : (k + 1) * share] = jnp.dot(
                embedded, wbuf[k], preferred_element_type=F32
            )
        give(step, 1).start()
        return 0

    lax.fori_loop(0, steps, make, 0)

    def finish(step, _):
        give(step, 0).wait()
        give(step, 1).wait()
        return 0

    lax.fori_loop(0, steps, finish, 0)


def full_lanes(part):
    rows = part.shape[0]
    if rows < 256:
        part = jnp.concatenate([part, jnp.zeros((256 - rows, 128), F32)], axis=0)
    return jnp.transpose(part)


def lanes_from_row(row, rows):
    return jnp.transpose(jnp.broadcast_to(row, (128, row.shape[1])))[:rows]


def gates_kernel(step, emb_hbm, x_hbm, w_ref, g_ref, stat_ref, x_ref, wbuf, sem):
    parts, depth, share = w_ref.shape
    chunks = depth // HID - 1
    per = HID // share

    def fetch(c):
        at = pl.ds(pl.multiple_of((c + 1) * HID, HID), HID)
        return pltpu.make_async_copy(w_ref.at[:, at, :], wbuf.at[c], sem.at[c])

    def fetch_x(c):
        at = pl.ds(c * per, per)
        return pltpu.make_async_copy(x_hbm.at[at], x_ref.at[at], sem.at[chunks + c])

    emb = pltpu.make_async_copy(emb_hbm.at[step], g_ref, sem.at[2 * chunks])
    fetch_x(0).start()
    fetch(0).start()
    emb.start()
    for c in range(1, chunks):
        fetch_x(c).start()
        fetch(c).start()
    emb.wait()

    def add(c, _):
        fetch_x(c).wait()
        left = jnp.concatenate([x_ref[c * per + q] for q in range(per)], axis=1)
        fetch(c).wait()
        for k in range(parts):
            g_ref[:, k * share : (k + 1) * share] += jnp.dot(
                left, wbuf[c, k], preferred_element_type=F32
            )
        return 0

    lax.fori_loop(0, chunks, add, 0)
    rows, width = g_ref.shape
    part = jnp.zeros((rows, 128), F32)
    part_sq = part
    for q in range(width // 128):
        piece = g_ref[:, q * 128 : (q + 1) * 128]
        part += piece
        part_sq += piece * piece
    sums = jnp.concatenate(
        [
            jnp.sum(full_lanes(part), axis=0, keepdims=True),
            jnp.sum(full_lanes(part_sq), axis=0, keepdims=True),
        ],
        axis=0,
    )
    for q in range(stat_ref.shape[0]):
        stat_ref[q] = sums


def spread_copies(low_ref, low_hbm, rows, sem):
    for k in range(low_hbm.shape[0]):
        pltpu.make_async_copy(low_ref.at[rows], low_hbm.at[k, rows], sem.at[k]).start()


def update_kernel(entries, step, g_ref, stat_ref, carried_ref, live_ref, new_ref, low_ref):
    sums = jnp.sum(stat_ref[...], axis=0) / entries
    avg = sums[0:1]
    inv = lax.rsqrt(sums[1:2] - avg * avg + 1e-5)
    rows, share = carried_ref.shape
    avg_l = lanes_from_row(avg, rows)
    inv_l = lanes_from_row(inv, rows)
    live_l = lanes_from_row(live_ref[pl.ds(step, 1), :], rows)
    for q in range(share // 128):
        def normed(part):
            at = part * share + q * 128
            return (g_ref[:, at : at + 128] - avg_l) * inv_l

        held = carried_ref[:, q * 128 : (q + 1) * 128]
        reset = sigmoid(normed(0))
        candidate = jnp.tanh(reset * normed(1))
        update = sigmoid(normed(2) - 1.0)
        renewed = update * candidate + (1.0 - update) * held
        renewed = jnp.where(live_l > 0, renewed, held)
        new_ref[:, q * 128 : (q + 1) * 128] = renewed
        low = renewed.astype(BF16)
        for k in range(low_ref.shape[0]):
            low_ref[k, :, q * 128 : (q + 1) * 128] = low


def two_parts(values):
    high = values.astype(BF16)
    return high, (values - high.astype(F32)).astype(BF16)


def prior_kernel(
    at_step, step, x_hbm, w_ref, logit_ref, head_ref, hot_hbm, live_ref, out_ref,
    x_ref, wbuf, lbuf, pre_ref, hid_ref, hot_ref, parts_ref, sem,
):
    shards, rows, share = x_ref.shape
    chunks = w_ref.shape[0] // HID
    per = HID // share

    def fetch(c):
        at = pl.ds(pl.multiple_of(c * HID, HID), HID)
        return pltpu.make_async_copy(w_ref.at[at], wbuf.at[c], sem.at[c])

    state = pltpu.make_async_copy(x_hbm, x_ref, sem.at[chunks + 2])
    state.start()
    for c in range(chunks):
        fetch(c).start()
    last = pltpu.make_async_copy(logit_ref, lbuf, sem.at[chunks])
    last.start()
    marks = pltpu.make_async_copy(hot_hbm.at[at_step], hot_ref, sem.at[chunks + 1])
    marks.start()
    pre_ref[...] = jnp.zeros(pre_ref.shape, F32)
    state.wait()

    def add(c, _):
        left = jnp.concatenate([x_ref[c * per + q] for q in range(per)], axis=1)
        fetch(c).wait()
        pre_ref[...] += jnp.dot(left, wbuf[c], preferred_element_type=F32)
        return 0

    lax.fori_loop(0, chunks, add, 0)

    def squash(k, _):
        at = pl.ds(pl.multiple_of(k * PIECE, PIECE), PIECE)
        hid_ref[at] = silu(row_norm(pre_ref[at])).astype(BF16)
        return 0

    lax.fori_loop(0, rows // PIECE, squash, 0)
    last.wait()
    marks.wait()
    across = (((1,), (1,)), ((), ()))
    heads = lax.dot_general(head_ref[...], hid_ref[...], across, preferred_element_type=F32)
    pre_ref[...] = jnp.dot(hid_ref[...], lbuf[...], preferred_element_type=F32)
    spread = spread_matrix()

    def classes(k, _):
        at = pl.ds(pl.multiple_of(k * PIECE, PIECE), PIECE)
        high, low = two_parts(jnp.exp(5.0 * jnp.tanh(pre_ref[at] / 5.0)))
        hot = hot_ref[at]
        parts_ref[0, at] = high
        parts_ref[1, at] = low
        parts_ref[2, at] = high * hot
        parts_ref[3, at] = low * hot
        return 0

    lax.fori_loop(0, rows // PIECE, classes, 0)

    def over_groups(k):
        return lax.dot_general(
            spread, parts_ref[k], across, preferred_element_type=F32
        ) + lax.dot_general(spread, parts_ref[k + 1], across, preferred_element_type=F32)

    chances = 0.99 * over_groups(2) / over_groups(0) + 0.01 / CLASSES
    log_prob = jnp.sum(jnp.log(chances), axis=0, keepdims=True)
    live = live_ref[pl.ds(step, 1), :rows]
    out_ref[...] = jnp.zeros(out_ref.shape, F32)
    out_ref[0:1, :rows] = log_prob * live
    out_ref[1:2, :rows] = heads[0:1] * live
    out_ref[2:3, :rows] = sigmoid(heads[1:2]) * live


def pick_kernel(at_ref, own_ref, other_ref, carried_ref, low_hbm, *refs):
    *rest, low_ref, sem = refs
    count, per_task, share = own_ref.shape
    done = carried_ref.shape[0] // per_task
    for i in range(count):
        at = at_ref[i]
        inner = at % count
        value = jnp.where(at < count, own_ref[inner], other_ref[inner])
        low = value.astype(BF16)
        rows = slice(i * per_task, (i + 1) * per_task)
        if i < done:
            carried_ref[rows] = value
            low_ref[rows] = low
        else:
            rest[0][(i - done) * per_task : (i - done + 1) * per_task] = low
        if i == done - 1:
            spread_copies(low_ref, low_hbm, pl.ds(0, done * per_task), sem)
    for k in range(low_hbm.shape[0]):
        pltpu.make_async_copy(low_ref, low_hbm.at[k], sem.at[k]).wait()


def settle_kernel(
    rows, at_ref, to_ref, got_ref, left_ref, outs_ref,
    log_ref, reward_ref, cont_ref, final_ref, buf, tall_ref, mine_ref, sem,
):
    count, per_task, share = buf.shape
    done = rows // per_task
    for i in range(count):
        chunk = at_ref[1, i]

        def bring(ref, chunk, i=i):
            at = pl.ds(pl.multiple_of(chunk * per_task, per_task), per_task)
            pltpu.make_async_copy(ref.at[at_ref[0, i], at], buf.at[i], sem.at[i]).start()

        if done == count:
            bring(got_ref, chunk)
        else:
            pl.when(chunk < done)(functools.partial(bring, got_ref, chunk))
            pl.when(chunk >= done)(functools.partial(bring, left_ref, chunk - done))

    holders, depth, lanes = outs_ref.shape
    half = depth // 2
    for d in range(holders):
        both = outs_ref[d].astype(F32)
        tall_ref[d * lanes : (d + 1) * lanes] = jnp.transpose(both[:half] + both[half:])
    for t in range(STEPS):
        for i in range(count):
            at = to_ref[t, i]
            from_rows = pl.ds(pl.multiple_of(jnp.maximum(at, 0), per_task), per_task)
            mine_ref[i * per_task : (i + 1) * per_task] = jnp.where(at >= 0, tall_ref[from_rows], 0.0)
        flat = jnp.transpose(mine_ref[...])
        for k, ref in enumerate((log_ref, reward_ref, cont_ref)):
            ref[t : t + 1] = flat[t * 3 + k : t * 3 + k + 1]
    for i in range(count):
        pltpu.make_async_copy(got_ref.at[0, pl.ds(0, per_task)], buf.at[i], sem.at[i]).wait()
        final_ref[i * per_task : (i + 1) * per_task] = buf[i].astype(F32)


def params(mib):
    return pltpu.CompilerParams(vmem_limit_bytes=mib * 1024 * 1024)


WHOLE = pl.BlockSpec()
STAY = pl.BlockSpec(memory_space=pltpu.HBM)
EITHER = pl.BlockSpec(memory_space=pl.ANY)
SCALARS = pl.BlockSpec(memory_space=pltpu.SMEM)


def placed(specs, operands):
    return tuple(
        pltpu.with_memory_space_constraint(o, pltpu.HBM) if s is STAY else o
        for s, o in zip(specs, operands, strict=True)
    )


def embed(first, steps, at, everyone, stoch, act, w, rows):
    depth = everyone.shape[2]
    parts, _, share = w.shape
    specs = [SCALARS, STAY, STAY, WHOLE, STAY]
    return pl.pallas_call(
        functools.partial(embed_kernel, first),
        in_specs=specs,
        out_specs=[STAY, STAY],
        out_shape=[
            pltpu.HBM((steps, rows, parts * share), F32),
            pltpu.HBM((steps, rows, HID), BF16),
        ],
        scratch_shapes=[
            pltpu.VMEM((steps, rows, depth), BF16),
            pltpu.VMEM(stoch.shape, BF16),
            pltpu.VMEM((parts, HID, share), BF16),
            pltpu.VMEM((steps, rows, HID), BF16),
            pltpu.VMEM((steps, rows, parts * share), F32),
            pltpu.SemaphoreType.DMA((steps, rows // PIECE)),
            pltpu.SemaphoreType.DMA((3, max(steps, 2))),
        ],
        compiler_params=params(24),
        name="embed",
    )(*placed(specs, (at, everyone, stoch, act, w)))


def stepped(kernel, steps, specs, operands):
    operands = placed(specs, operands)
    if all(isinstance(step, int) for step in steps):
        return functools.partial(kernel, *steps), specs, operands

    def with_scalars(step_ref, *refs):
        kernel(*(step_ref[k] for k in range(len(steps))), *refs)

    return with_scalars, [SCALARS, *specs], (jnp.stack(steps), *operands)


def gates(at, emb, x, w):
    kernel, specs, operands = stepped(gates_kernel, (at,), [STAY, EITHER, STAY], (emb, x, w))
    shards, rows, share = x.shape
    parts, depth, _ = w.shape
    return pl.pallas_call(
        kernel,
        in_specs=specs,
        out_shape=[
            jax.ShapeDtypeStruct((rows, parts * share), F32),
            jax.ShapeDtypeStruct((shards, 2, 256), F32),
        ],
        scratch_shapes=[
            pltpu.VMEM(x.shape, BF16),
            pltpu.VMEM((depth // HID - 1, parts, HID, share), BF16),
            pltpu.SemaphoreType.DMA((2 * (depth // HID) - 1,)),
        ],
        compiler_params=params(24),
        name="gates",
    )(*operands)


def renew(moment, g, stats, carried, live, entries, copies):
    kernel, specs, operands = stepped(
        functools.partial(update_kernel, entries), (moment,), [WHOLE] * 4, (g, stats, carried, live)
    )
    rows, share = carried.shape
    return pl.pallas_call(
        kernel,
        in_specs=specs,
        out_shape=[
            jax.ShapeDtypeStruct((rows, share), F32),
            jax.ShapeDtypeStruct((copies, rows, share), BF16),
        ],
        compiler_params=params(16),
        name="renew",
    )(*operands)


def prior(at, moment, x, w, logit, head, hot, live):
    kernel, specs, operands = stepped(
        prior_kernel,
        (at, moment),
        [STAY, STAY, STAY, WHOLE, STAY, WHOLE],
        (x, w, logit, head, hot, live),
    )
    rows = x.shape[1]
    chunks = w.shape[0] // HID
    return pl.pallas_call(
        kernel,
        in_specs=specs,
        out_shape=jax.ShapeDtypeStruct((8, 256), F32),
        scratch_shapes=[
            pltpu.VMEM(x.shape, BF16),
            pltpu.VMEM((chunks, HID, HID), BF16),
            pltpu.VMEM((HID, HID), BF16),
            pltpu.VMEM((rows, HID), F32),
            pltpu.VMEM((rows, HID), BF16),
            pltpu.VMEM((rows, HID), BF16),
            pltpu.VMEM((4, rows, HID), BF16),
            pltpu.SemaphoreType.DMA((chunks + 3,)),
        ],
        compiler_params=params(28),
        name="prior",
    )(*operands)


def pick(at, own, other, rows, shards):
    count, per_task, share = own.shape
    left = count * per_task - rows
    shapes = [
        jax.ShapeDtypeStruct((rows, share), F32),
        pltpu.HBM((shards, rows, share), BF16),
    ]
    if left:
        shapes.append(jax.ShapeDtypeStruct((left, share), BF16))
    return pl.pallas_call(
        pick_kernel,
        in_specs=[SCALARS, WHOLE, WHOLE],
        out_shape=shapes,
        out_specs=[WHOLE, STAY] + [WHOLE] * (len(shapes) - 2),
        scratch_shapes=[pltpu.VMEM((rows, share), BF16), pltpu.SemaphoreType.DMA((shards,))],
        compiler_params=params(16),
        name="pick",
    )(at, own, other)


def settle(at, to, got, left, outs, rows, count, per_task):
    share = got.shape[2]
    holders, depth, lanes = outs.shape
    return pl.pallas_call(
        functools.partial(settle_kernel, rows),
        in_specs=[SCALARS, SCALARS, EITHER, EITHER, WHOLE],
        out_shape=[jax.ShapeDtypeStruct((STEPS, count * per_task), F32)] * 3
        + [jax.ShapeDtypeStruct((count * per_task, share), F32)],
        scratch_shapes=[
            pltpu.VMEM((count, per_task, share), BF16),
            pltpu.VMEM((holders * lanes, depth // 2), F32),
            pltpu.VMEM((count * per_task, depth // 2), F32),
            pltpu.SemaphoreType.DMA((count,)),
        ],
        compiler_params=params(16),
        name="settle",
    )(at, to, got, left, outs)


def exchange(copies, axis):
    return lax.all_to_all(copies, axis, 0, 0, tiled=True)


def window(count, args, holders, shards):
    (
        deter, other, draws, actions, horizons, offsets, rank, local, from_task,
        stoch, act, w, prior_weight, logit, head,
    ) = args
    all_rows, share = deter.shape
    per_core = local.shape[0]
    per_task = all_rows // per_core
    rows = count * per_task
    entries = 3 * share * shards
    place = lax.axis_index("task")
    pair = 2 * per_core
    in_block = per_core // BLK_DEV

    carried, low, *rest = pick(
        from_task,
        deter.reshape(per_core, per_task, share),
        other.reshape(per_core, per_task, share),
        rows,
        shards,
    )
    x = exchange(low, "mp")

    sent = jnp.concatenate([draws, actions[:, None]], axis=1).astype(BF16)
    sent = jnp.concatenate([sent.reshape(STEPS * DEPTH, all_rows), *rest], axis=0)
    everyone = lax.all_gather(sent, "task")
    left = everyone[:, STEPS * DEPTH :]
    everyone = everyone[:, : STEPS * DEPTH].reshape(holders, STEPS, DEPTH, all_rows)
    everyone = jnp.transpose(everyone, (1, 0, 3, 2)).reshape(STEPS, holders * all_rows, DEPTH)

    task = place // 2 * pair + local
    horizon = jnp.sum(
        jnp.where(task[:, None] == jnp.arange(TASKS, dtype=I32)[None, :], horizons[None, :], 0), axis=1
    )
    moments = WSTART + jnp.arange(STEPS, dtype=I32)
    living = jnp.repeat((horizon[None, :] > moments[:, None]).astype(F32), per_task, axis=1)

    running = jnp.cumsum(offsets, axis=0) % holders
    lane_block = task % per_core // in_block
    blocks = jnp.arange(BLK_DEV, dtype=I32)
    ahead_by = jnp.sum(
        jnp.where(lane_block[None, :, None] == blocks, running[:, None, :], 0), axis=2
    )
    slot = (task[None, :] // per_core + ahead_by) % holders
    source = slot * all_rows + (task % per_core)[None, :] * per_task
    first = STEPS if count in ROLLED else 1
    emb, hot = embed(0, first, source, everyone, stoch, act, w, rows)
    x, emb, hot = lax.optimization_barrier((x, emb, hot))

    held = jnp.repeat((place - running) % holders, in_block, axis=1) * per_core
    held = held + jnp.arange(per_core, dtype=I32)[None, :]
    dealt = jnp.sum(
        jnp.where(held[:, :, None] == jnp.arange(TASKS, dtype=I32), rank.reshape(-1), 0), axis=2
    )
    core = held // pair * 2 + dealt % 2
    chunk = dealt // 2
    settle_at = jnp.stack([core[STEPS - 1], chunk[STEPS - 1]])
    to = jnp.where(chunk < count, core * share + chunk * per_task, -1)

    def likely(at, moment, x, hot):
        return prior(at, moment, x, prior_weight, logit, head, hot, living)[:3]

    def gated(at, moment, x, emb, carried):
        g, stats = gates(at, emb, x, w)
        stats = exchange(stats, "mp")
        return renew(moment, g, stats, carried, living, entries, shards)

    small = []
    if count in ROLLED:

        def body(state, moment):
            x, carried = state
            carried, low = gated(moment, moment, x, emb, carried)
            out = likely(moment, moment, x, hot)
            x, out = lax.optimization_barrier((exchange(low, "mp"), out))
            return (x, carried), out

        (x, carried), outs = lax.scan(body, (x, carried), jnp.arange(STEPS - 1, dtype=I32))
        small.append(outs.reshape(-1, outs.shape[2]))
        at = STEPS - 1
    else:
        at = 0
        for moment in range(STEPS - 1):
            carried, low = gated(at, moment, x, emb, carried)
            out = likely(at, moment, x, hot)
            if moment == 0:
                emb, hot = embed(1, STEPS - 1, source, everyone, stoch, act, w, rows)
            x = exchange(low, "mp")
            x, out, emb, hot = lax.optimization_barrier((x, out, emb, hot))
            small.append(out)
            at = moment

    g, stats = gates(at, emb, x, w)
    stats = exchange(stats, "mp")
    out = likely(at, STEPS - 1, x, hot)
    stats, small, out = lax.optimization_barrier((stats, small, out))
    _, low = renew(STEPS - 1, g, stats, carried, living, entries, 1)

    outs = jnp.concatenate([*small, out], axis=0)
    high, low_part = two_parts(outs)
    pad = jnp.zeros((16 - high.shape[0], share), BF16)
    sent = jnp.concatenate([low[0], high, pad, low_part, pad], axis=0)
    got = exchange(jnp.broadcast_to(sent[None], (holders, *sent.shape)), "task")
    outs = got[:, rows:]
    if not rest:
        left = got
    return settle(settle_at, to, got, left, outs, rows, per_core, per_task)


def on_device(
    deter,
    draws,
    actions,
    horizons,
    offsets,
    embed_stoch,
    embed_act,
    gru_weight,
    prior_weight,
    logit_weight,
    head_weight,
):
    holders = lax.axis_size("task")
    place = lax.axis_index("task")
    shards = lax.axis_size("mp")
    rows, share = deter.shape
    per_core = TASKS // holders
    pair = 2 * per_core

    other = lax.ppermute(deter, "task", [(i, i ^ 1) for i in range(holders)])
    w = jnp.transpose(gru_weight, (1, 0, 2))
    head = jnp.transpose(head_weight)

    by_chip = horizons.reshape(TASKS // pair, pair)
    index = jnp.arange(pair, dtype=I32)
    ahead = (by_chip[:, None, :] > by_chip[:, :, None]) | (
        (by_chip[:, None, :] == by_chip[:, :, None]) & (index[None, None, :] < index[None, :, None])
    )
    rank = jnp.sum(ahead.astype(I32), axis=2)
    most = jnp.max(jnp.sum((by_chip > WSTART).astype(I32), axis=1))
    need = (most + 1) // 2
    level = sum((need > n).astype(I32) for n in LEVELS[:-1])

    chip = place // 2
    mine = 2 * jnp.arange(per_core, dtype=I32) + place % 2
    my_rank = jnp.sum(
        jnp.where(jnp.arange(TASKS // pair, dtype=I32)[:, None] == chip, rank, 0), axis=0
    )
    local = jnp.sum(jnp.where(my_rank[None, :] == mine[:, None], index[None, :], 0), axis=1)
    swapped = (local // per_core != place % 2).astype(I32)
    from_task = swapped * per_core + local % per_core
    operands = (
        deter, other, draws, actions, horizons, offsets, rank, local, from_task,
        embed_stoch, embed_act, w, prior_weight, logit_weight, head,
    )
    branches = [lambda args, n=n: window(n, args, holders, shards) for n in LEVELS]
    return tuple(lax.switch(level, branches, operands))


def solution(mesh):
    in_specs = (
        P("task", "mp"),
        P(None, None, "task"),
        P(None, "task"),
        P(),
        P(),
        P(),
        P(),
        P(None, None, "mp"),
        P(),
        P(),
        P(),
    )
    out_specs = (P(None, "task"), P(None, "task"), P(None, "task"), P("task", "mp"))
    return jax.shard_map(
        on_device, mesh=mesh, in_specs=in_specs, out_specs=out_specs, check_vma=False
    )
```

```python
import functools

import jax
import jax.numpy as jnp
from jax import lax
from jax.experimental import pallas as pl
from jax.experimental.pallas import tpu as pltpu
from jax.sharding import PartitionSpec as P

HID = 1024
GROUPS = 32
CLASSES = 32
TASKS = 64
BLK_DEV = 4
STEPS = 4
WSTART = 16
DEPTH = GROUPS + 1
LEVELS = (6, 8)
PIECE = 32
ROLLED = (8,)
F32 = jnp.float32
BF16 = jnp.bfloat16
I32 = jnp.int32


def silu(v):
    return v * sigmoid(v)


def sigmoid(v):
    return 0.5 + 0.5 * jnp.tanh(0.5 * v)


def row_norm(pre):
    entries = pre.shape[1]
    avg = jnp.sum(pre, axis=1, keepdims=True) / entries
    squares = jnp.sum(pre * pre, axis=1, keepdims=True) / entries
    return (pre - avg) * lax.rsqrt(squares - avg * avg + 1e-5)


def spread_matrix():
    variable = lax.broadcasted_iota(I32, (GROUPS, HID), 0)
    entry = lax.broadcasted_iota(I32, (GROUPS, HID), 1)
    return (entry // CLASSES == variable).astype(F32).astype(BF16)


def chosen_mask(by_row, spread):
    wide = jnp.dot(by_row, spread, preferred_element_type=F32)
    entry = lax.broadcasted_iota(I32, wide.shape, 1)
    return wide == (entry % CLASSES).astype(F32)


def embed_kernel(
    first, at_ref, ev_hbm, stoch_hbm, act_ref, w_hbm, out_hbm, hot_hbm,
    picks_ref, stoch_ref, wbuf, hot_ref, out_ref, sem, done_sem,
):
    steps, rows, _ = hot_ref.shape
    count = rows // PIECE

    def fetch(step, k):
        at = pl.ds(pl.multiple_of(at_ref[first + step, k], PIECE), PIECE)
        to = pl.ds(k * PIECE, PIECE)
        return pltpu.make_async_copy(
            ev_hbm.at[first + step, at], picks_ref.at[step, to], sem.at[step, k]
        )

    def give(step, q):
        ref, hbm = ((hot_ref, hot_hbm), (out_ref, out_hbm))[q]
        return pltpu.make_async_copy(ref.at[step], hbm.at[step], done_sem.at[q, step])

    def start(step, _):
        for k in range(count):
            fetch(step, k).start()
        return 0

    lax.fori_loop(0, steps, start, 0)
    table = pltpu.make_async_copy(stoch_hbm, stoch_ref, done_sem.at[2, 0])
    table.start()
    weights = pltpu.make_async_copy(w_hbm.at[:, pl.ds(0, HID), :], wbuf, done_sem.at[2, 1])
    weights.start()
    spread = spread_matrix()
    ids = lax.broadcasted_iota(I32, (rows, act_ref.shape[0]), 1).astype(F32)

    def make(step, _):
        for k in range(count):
            fetch(step, k).wait()
        wanted = picks_ref[step]
        hot = chosen_mask(wanted[:, :GROUPS], spread).astype(F32).astype(BF16)
        hot_ref[step] = hot
        give(step, 0).start()

        @pl.when(step == 0)
        def _():
            table.wait()

        action = wanted[:, GROUPS : GROUPS + 1].astype(F32)
        act_hot = (ids == action).astype(F32).astype(BF16)
        pre = jnp.dot(hot, stoch_ref[...], preferred_element_type=F32) + jnp.dot(
            act_hot, act_ref[...], preferred_element_type=F32
        )
        embedded = silu(row_norm(pre)).astype(BF16)

        @pl.when(step == 0)
        def _():
            weights.wait()

        share = wbuf.shape[2]
        for k in range(wbuf.shape[0]):
            out_ref[step, :, k * share : (k + 1) * share] = jnp.dot(
                embedded, wbuf[k], preferred_element_type=F32
            )
        give(step, 1).start()
        return 0

    lax.fori_loop(0, steps, make, 0)

    def finish(step, _):
        give(step, 0).wait()
        give(step, 1).wait()
        return 0

    lax.fori_loop(0, steps, finish, 0)


def full_lanes(part):
    rows = part.shape[0]
    if rows < 256:
        part = jnp.concatenate([part, jnp.zeros((256 - rows, 128), F32)], axis=0)
    return jnp.transpose(part)


def lanes_from_row(row, rows):
    return jnp.transpose(jnp.broadcast_to(row, (128, row.shape[1])))[:rows]


def gates_kernel(step, emb_hbm, x_hbm, w_ref, g_ref, stat_ref, x_ref, wbuf, sem):
    parts, depth, share = w_ref.shape
    chunks = depth // HID - 1
    per = HID // share

    def fetch(c):
        at = pl.ds(pl.multiple_of((c + 1) * HID, HID), HID)
        return pltpu.make_async_copy(w_ref.at[:, at, :], wbuf.at[c], sem.at[c])

    def fetch_x(c):
        at = pl.ds(c * per, per)
        return pltpu.make_async_copy(x_hbm.at[at], x_ref.at[at], sem.at[chunks + c])

    emb = pltpu.make_async_copy(emb_hbm.at[step], g_ref, sem.at[2 * chunks])
    fetch_x(0).start()
    fetch(0).start()
    emb.start()
    for c in range(1, chunks):
        fetch_x(c).start()
        fetch(c).start()
    emb.wait()

    def add(c, _):
        fetch_x(c).wait()
        left = jnp.concatenate([x_ref[c * per + q] for q in range(per)], axis=1)
        fetch(c).wait()
        for k in range(parts):
            g_ref[:, k * share : (k + 1) * share] += jnp.dot(
                left, wbuf[c, k], preferred_element_type=F32
            )
        return 0

    lax.fori_loop(0, chunks, add, 0)
    rows, width = g_ref.shape
    part = jnp.zeros((rows, 128), F32)
    part_sq = part
    for q in range(width // 128):
        piece = g_ref[:, q * 128 : (q + 1) * 128]
        part += piece
        part_sq += piece * piece
    sums = jnp.concatenate(
        [
            jnp.sum(full_lanes(part), axis=0, keepdims=True),
            jnp.sum(full_lanes(part_sq), axis=0, keepdims=True),
        ],
        axis=0,
    )
    for q in range(stat_ref.shape[0]):
        stat_ref[q] = sums


def spread_copies(low_ref, low_hbm, rows, sem):
    for k in range(low_hbm.shape[0]):
        pltpu.make_async_copy(low_ref.at[rows], low_hbm.at[k, rows], sem.at[k]).start()


def update_kernel(entries, step, g_ref, stat_ref, carried_ref, live_ref, new_ref, low_ref):
    sums = jnp.sum(stat_ref[...], axis=0) / entries
    avg = sums[0:1]
    inv = lax.rsqrt(sums[1:2] - avg * avg + 1e-5)
    rows, share = carried_ref.shape
    avg_l = lanes_from_row(avg, rows)
    inv_l = lanes_from_row(inv, rows)
    live_l = lanes_from_row(live_ref[pl.ds(step, 1), :], rows)
    for q in range(share // 128):
        def normed(part):
            at = part * share + q * 128
            return (g_ref[:, at : at + 128] - avg_l) * inv_l

        held = carried_ref[:, q * 128 : (q + 1) * 128]
        reset = sigmoid(normed(0))
        candidate = jnp.tanh(reset * normed(1))
        update = sigmoid(normed(2) - 1.0)
        renewed = update * candidate + (1.0 - update) * held
        renewed = jnp.where(live_l > 0, renewed, held)
        new_ref[:, q * 128 : (q + 1) * 128] = renewed
        low = renewed.astype(BF16)
        for k in range(low_ref.shape[0]):
            low_ref[k, :, q * 128 : (q + 1) * 128] = low


def two_parts(values):
    high = values.astype(BF16)
    return high, (values - high.astype(F32)).astype(BF16)


def prior_kernel(
    at_step, step, x_hbm, w_ref, logit_ref, head_ref, hot_hbm, live_ref, out_ref,
    x_ref, wbuf, lbuf, pre_ref, hid_ref, hot_ref, parts_ref, sem,
):
    shards, rows, share = x_ref.shape
    chunks = w_ref.shape[0] // HID
    per = HID // share

    def fetch(c):
        at = pl.ds(pl.multiple_of(c * HID, HID), HID)
        return pltpu.make_async_copy(w_ref.at[at], wbuf.at[c], sem.at[c])

    state = pltpu.make_async_copy(x_hbm, x_ref, sem.at[chunks + 2])
    state.start()
    for c in range(chunks):
        fetch(c).start()
    last = pltpu.make_async_copy(logit_ref, lbuf, sem.at[chunks])
    last.start()
    marks = pltpu.make_async_copy(hot_hbm.at[at_step], hot_ref, sem.at[chunks + 1])
    marks.start()
    pre_ref[...] = jnp.zeros(pre_ref.shape, F32)
    state.wait()

    def add(c, _):
        left = jnp.concatenate([x_ref[c * per + q] for q in range(per)], axis=1)
        fetch(c).wait()
        pre_ref[...] += jnp.dot(left, wbuf[c], preferred_element_type=F32)
        return 0

    lax.fori_loop(0, chunks, add, 0)

    def squash(k, _):
        at = pl.ds(pl.multiple_of(k * PIECE, PIECE), PIECE)
        hid_ref[at] = silu(row_norm(pre_ref[at])).astype(BF16)
        return 0

    lax.fori_loop(0, rows // PIECE, squash, 0)
    last.wait()
    marks.wait()
    across = (((1,), (1,)), ((), ()))
    heads = lax.dot_general(head_ref[...], hid_ref[...], across, preferred_element_type=F32)
    pre_ref[...] = jnp.dot(hid_ref[...], lbuf[...], preferred_element_type=F32)
    spread = spread_matrix()

    def classes(k, _):
        at = pl.ds(pl.multiple_of(k * PIECE, PIECE), PIECE)
        high, low = two_parts(jnp.exp(5.0 * jnp.tanh(pre_ref[at] / 5.0)))
        hot = hot_ref[at]
        parts_ref[0, at] = high
        parts_ref[1, at] = low
        parts_ref[2, at] = high * hot
        parts_ref[3, at] = low * hot
        return 0

    lax.fori_loop(0, rows // PIECE, classes, 0)

    def over_groups(k):
        return lax.dot_general(
            spread, parts_ref[k], across, preferred_element_type=F32
        ) + lax.dot_general(spread, parts_ref[k + 1], across, preferred_element_type=F32)

    chances = 0.99 * over_groups(2) / over_groups(0) + 0.01 / CLASSES
    log_prob = jnp.sum(jnp.log(chances), axis=0, keepdims=True)
    live = live_ref[pl.ds(step, 1), :rows]
    out_ref[...] = jnp.zeros(out_ref.shape, F32)
    out_ref[0:1, :rows] = log_prob * live
    out_ref[1:2, :rows] = heads[0:1] * live
    out_ref[2:3, :rows] = sigmoid(heads[1:2]) * live


def pick_kernel(at_ref, own_ref, other_ref, carried_ref, low_hbm, *refs):
    *rest, low_ref, sem = refs
    count, per_task, share = own_ref.shape
    done = carried_ref.shape[0] // per_task
    for i in range(count):
        at = at_ref[i]
        inner = at % count
        value = jnp.where(at < count, own_ref[inner], other_ref[inner])
        low = value.astype(BF16)
        rows = slice(i * per_task, (i + 1) * per_task)
        if i < done:
            carried_ref[rows] = value
            low_ref[rows] = low
        else:
            rest[0][(i - done) * per_task : (i - done + 1) * per_task] = low
        if i == done - 1:
            spread_copies(low_ref, low_hbm, pl.ds(0, done * per_task), sem)
    for k in range(low_hbm.shape[0]):
        pltpu.make_async_copy(low_ref, low_hbm.at[k], sem.at[k]).wait()


def settle_kernel(
    rows, at_ref, to_ref, got_ref, left_ref, outs_ref,
    log_ref, reward_ref, cont_ref, final_ref, buf, tall_ref, mine_ref, sem,
):
    count, per_task, share = buf.shape
    done = rows // per_task
    for i in range(count):
        chunk = at_ref[1, i]

        def bring(ref, chunk, i=i):
            at = pl.ds(pl.multiple_of(chunk * per_task, per_task), per_task)
            pltpu.make_async_copy(ref.at[at_ref[0, i], at], buf.at[i], sem.at[i]).start()

        if done == count:
            bring(got_ref, chunk)
        else:
            pl.when(chunk < done)(functools.partial(bring, got_ref, chunk))
            pl.when(chunk >= done)(functools.partial(bring, left_ref, chunk - done))

    holders, depth, lanes = outs_ref.shape
    half = depth // 2
    for d in range(holders):
        both = outs_ref[d].astype(F32)
        tall_ref[d * lanes : (d + 1) * lanes] = jnp.transpose(both[:half] + both[half:])
    for t in range(STEPS):
        for i in range(count):
            at = to_ref[t, i]
            from_rows = pl.ds(pl.multiple_of(jnp.maximum(at, 0), per_task), per_task)
            mine_ref[i * per_task : (i + 1) * per_task] = jnp.where(at >= 0, tall_ref[from_rows], 0.0)
        flat = jnp.transpose(mine_ref[...])
        for k, ref in enumerate((log_ref, reward_ref, cont_ref)):
            ref[t : t + 1] = flat[t * 3 + k : t * 3 + k + 1]
    for i in range(count):
        pltpu.make_async_copy(got_ref.at[0, pl.ds(0, per_task)], buf.at[i], sem.at[i]).wait()
        final_ref[i * per_task : (i + 1) * per_task] = buf[i].astype(F32)


def params(mib):
    return pltpu.CompilerParams(vmem_limit_bytes=mib * 1024 * 1024)


WHOLE = pl.BlockSpec()
STAY = pl.BlockSpec(memory_space=pltpu.HBM)
EITHER = pl.BlockSpec(memory_space=pl.ANY)
SCALARS = pl.BlockSpec(memory_space=pltpu.SMEM)


def placed(specs, operands):
    return tuple(
        pltpu.with_memory_space_constraint(o, pltpu.HBM) if s is STAY else o
        for s, o in zip(specs, operands, strict=True)
    )


def embed(first, steps, at, everyone, stoch, act, w, rows):
    depth = everyone.shape[2]
    parts, _, share = w.shape
    specs = [SCALARS, STAY, STAY, WHOLE, STAY]
    return pl.pallas_call(
        functools.partial(embed_kernel, first),
        in_specs=specs,
        out_specs=[STAY, STAY],
        out_shape=[
            pltpu.HBM((steps, rows, parts * share), F32),
            pltpu.HBM((steps, rows, HID), BF16),
        ],
        scratch_shapes=[
            pltpu.VMEM((steps, rows, depth), BF16),
            pltpu.VMEM(stoch.shape, BF16),
            pltpu.VMEM((parts, HID, share), BF16),
            pltpu.VMEM((steps, rows, HID), BF16),
            pltpu.VMEM((steps, rows, parts * share), F32),
            pltpu.SemaphoreType.DMA((steps, rows // PIECE)),
            pltpu.SemaphoreType.DMA((3, max(steps, 2))),
        ],
        compiler_params=params(24),
        name="embed",
    )(*placed(specs, (at, everyone, stoch, act, w)))


def stepped(kernel, steps, specs, operands):
    operands = placed(specs, operands)
    if all(isinstance(step, int) for step in steps):
        return functools.partial(kernel, *steps), specs, operands

    def with_scalars(step_ref, *refs):
        kernel(*(step_ref[k] for k in range(len(steps))), *refs)

    return with_scalars, [SCALARS, *specs], (jnp.stack(steps), *operands)


def gates(at, emb, x, w):
    kernel, specs, operands = stepped(gates_kernel, (at,), [STAY, EITHER, STAY], (emb, x, w))
    shards, rows, share = x.shape
    parts, depth, _ = w.shape
    return pl.pallas_call(
        kernel,
        in_specs=specs,
        out_shape=[
            jax.ShapeDtypeStruct((rows, parts * share), F32),
            jax.ShapeDtypeStruct((shards, 2, 256), F32),
        ],
        scratch_shapes=[
            pltpu.VMEM(x.shape, BF16),
            pltpu.VMEM((depth // HID - 1, parts, HID, share), BF16),
            pltpu.SemaphoreType.DMA((2 * (depth // HID) - 1,)),
        ],
        compiler_params=params(24),
        name="gates",
    )(*operands)


def renew(moment, g, stats, carried, live, entries, copies):
    kernel, specs, operands = stepped(
        functools.partial(update_kernel, entries), (moment,), [WHOLE] * 4, (g, stats, carried, live)
    )
    rows, share = carried.shape
    return pl.pallas_call(
        kernel,
        in_specs=specs,
        out_shape=[
            jax.ShapeDtypeStruct((rows, share), F32),
            jax.ShapeDtypeStruct((copies, rows, share), BF16),
        ],
        compiler_params=params(16),
        name="renew",
    )(*operands)


def prior(at, moment, x, w, logit, head, hot, live):
    kernel, specs, operands = stepped(
        prior_kernel,
        (at, moment),
        [STAY, STAY, STAY, WHOLE, STAY, WHOLE],
        (x, w, logit, head, hot, live),
    )
    rows = x.shape[1]
    chunks = w.shape[0] // HID
    return pl.pallas_call(
        kernel,
        in_specs=specs,
        out_shape=jax.ShapeDtypeStruct((8, 256), F32),
        scratch_shapes=[
            pltpu.VMEM(x.shape, BF16),
            pltpu.VMEM((chunks, HID, HID), BF16),
            pltpu.VMEM((HID, HID), BF16),
            pltpu.VMEM((rows, HID), F32),
            pltpu.VMEM((rows, HID), BF16),
            pltpu.VMEM((rows, HID), BF16),
            pltpu.VMEM((4, rows, HID), BF16),
            pltpu.SemaphoreType.DMA((chunks + 3,)),
        ],
        compiler_params=params(28),
        name="prior",
    )(*operands)


def pick(at, own, other, rows, shards):
    count, per_task, share = own.shape
    left = count * per_task - rows
    shapes = [
        jax.ShapeDtypeStruct((rows, share), F32),
        pltpu.HBM((shards, rows, share), BF16),
    ]
    if left:
        shapes.append(jax.ShapeDtypeStruct((left, share), BF16))
    return pl.pallas_call(
        pick_kernel,
        in_specs=[SCALARS, WHOLE, WHOLE],
        out_shape=shapes,
        out_specs=[WHOLE, STAY] + [WHOLE] * (len(shapes) - 2),
        scratch_shapes=[pltpu.VMEM((rows, share), BF16), pltpu.SemaphoreType.DMA((shards,))],
        compiler_params=params(16),
        name="pick",
    )(at, own, other)


def settle(at, to, got, left, outs, rows, count, per_task):
    share = got.shape[2]
    holders, depth, lanes = outs.shape
    return pl.pallas_call(
        functools.partial(settle_kernel, rows),
        in_specs=[SCALARS, SCALARS, EITHER, EITHER, WHOLE],
        out_shape=[jax.ShapeDtypeStruct((STEPS, count * per_task), F32)] * 3
        + [jax.ShapeDtypeStruct((count * per_task, share), F32)],
        scratch_shapes=[
            pltpu.VMEM((count, per_task, share), BF16),
            pltpu.VMEM((holders * lanes, depth // 2), F32),
            pltpu.VMEM((count * per_task, depth // 2), F32),
            pltpu.SemaphoreType.DMA((count,)),
        ],
        compiler_params=params(16),
        name="settle",
    )(at, to, got, left, outs)


def exchange(copies, axis):
    return lax.all_to_all(copies, axis, 0, 0, tiled=True)


def window(count, args, holders, shards):
    (
        deter, other, draws, actions, horizons, offsets, rank, local, from_task,
        stoch, act, w, prior_weight, logit, head,
    ) = args
    all_rows, share = deter.shape
    per_core = local.shape[0]
    per_task = all_rows // per_core
    rows = count * per_task
    entries = 3 * share * shards
    place = lax.axis_index("task")
    pair = 2 * per_core
    in_block = per_core // BLK_DEV

    carried, low, *rest = pick(
        from_task,
        deter.reshape(per_core, per_task, share),
        other.reshape(per_core, per_task, share),
        rows,
        shards,
    )
    x = exchange(low, "mp")

    sent = jnp.concatenate([draws, actions[:, None]], axis=1).astype(BF16)
    sent = jnp.concatenate([sent.reshape(STEPS * DEPTH, all_rows), *rest], axis=0)
    everyone = lax.all_gather(sent, "task")
    left = everyone[:, STEPS * DEPTH :]
    everyone = everyone[:, : STEPS * DEPTH].reshape(holders, STEPS, DEPTH, all_rows)
    everyone = jnp.transpose(everyone, (1, 0, 3, 2)).reshape(STEPS, holders * all_rows, DEPTH)

    task = place // 2 * pair + local
    horizon = jnp.sum(
        jnp.where(task[:, None] == jnp.arange(TASKS, dtype=I32)[None, :], horizons[None, :], 0), axis=1
    )
    moments = WSTART + jnp.arange(STEPS, dtype=I32)
    living = jnp.repeat((horizon[None, :] > moments[:, None]).astype(F32), per_task, axis=1)

    running = jnp.cumsum(offsets, axis=0) % holders
    lane_block = task % per_core // in_block
    blocks = jnp.arange(BLK_DEV, dtype=I32)
    ahead_by = jnp.sum(
        jnp.where(lane_block[None, :, None] == blocks, running[:, None, :], 0), axis=2
    )
    slot = (task[None, :] // per_core + ahead_by) % holders
    source = slot * all_rows + (task % per_core)[None, :] * per_task
    first = STEPS if count in ROLLED else 1
    emb, hot = embed(0, first, source, everyone, stoch, act, w, rows)
    x, emb, hot = lax.optimization_barrier((x, emb, hot))

    held = jnp.repeat((place - running) % holders, in_block, axis=1) * per_core
    held = held + jnp.arange(per_core, dtype=I32)[None, :]
    dealt = jnp.sum(
        jnp.where(held[:, :, None] == jnp.arange(TASKS, dtype=I32), rank.reshape(-1), 0), axis=2
    )
    core = held // pair * 2 + dealt % 2
    chunk = dealt // 2
    settle_at = jnp.stack([core[STEPS - 1], chunk[STEPS - 1]])
    to = jnp.where(chunk < count, core * share + chunk * per_task, -1)

    def likely(at, moment, x, hot):
        return prior(at, moment, x, prior_weight, logit, head, hot, living)[:3]

    def gated(at, moment, x, emb, carried):
        g, stats = gates(at, emb, x, w)
        stats = exchange(stats, "mp")
        return renew(moment, g, stats, carried, living, entries, shards)

    small = []
    if count in ROLLED:

        def body(state, moment):
            x, carried = state
            carried, low = gated(moment, moment, x, emb, carried)
            out = likely(moment, moment, x, hot)
            x, out = lax.optimization_barrier((exchange(low, "mp"), out))
            return (x, carried), out

        (x, carried), outs = lax.scan(body, (x, carried), jnp.arange(STEPS - 1, dtype=I32))
        small.append(outs.reshape(-1, outs.shape[2]))
        at = STEPS - 1
    else:
        at = 0
        for moment in range(STEPS - 1):
            carried, low = gated(at, moment, x, emb, carried)
            out = likely(at, moment, x, hot)
            if moment == 0:
                emb, hot = embed(1, STEPS - 1, source, everyone, stoch, act, w, rows)
            x = exchange(low, "mp")
            x, out, emb, hot = lax.optimization_barrier((x, out, emb, hot))
            small.append(out)
            at = moment

    g, stats = gates(at, emb, x, w)
    stats = exchange(stats, "mp")
    out = likely(at, STEPS - 1, x, hot)
    stats, small, out = lax.optimization_barrier((stats, small, out))
    _, low = renew(STEPS - 1, g, stats, carried, living, entries, 1)

    outs = jnp.concatenate([*small, out], axis=0)
    high, low_part = two_parts(outs)
    pad = jnp.zeros((16 - high.shape[0], share), BF16)
    sent = jnp.concatenate([low[0], high, pad, low_part, pad], axis=0)
    if count in ROLLED:
        got = exchange(jnp.broadcast_to(sent[None], (holders, *sent.shape)), "task")
    else:
        got = lax.all_gather(sent, "task")
    outs = got[:, rows:]
    if not rest:
        left = got
    return settle(settle_at, to, got, left, outs, rows, per_core, per_task)


def on_device(
    deter,
    draws,
    actions,
    horizons,
    offsets,
    embed_stoch,
    embed_act,
    gru_weight,
    prior_weight,
    logit_weight,
    head_weight,
):
    holders = lax.axis_size("task")
    place = lax.axis_index("task")
    shards = lax.axis_size("mp")
    rows, share = deter.shape
    per_core = TASKS // holders
    pair = 2 * per_core

    other = lax.ppermute(deter, "task", [(i, i ^ 1) for i in range(holders)])
    w = jnp.transpose(gru_weight, (1, 0, 2))
    head = jnp.transpose(head_weight)

    by_chip = horizons.reshape(TASKS // pair, pair)
    index = jnp.arange(pair, dtype=I32)
    ahead = (by_chip[:, None, :] > by_chip[:, :, None]) | (
        (by_chip[:, None, :] == by_chip[:, :, None]) & (index[None, None, :] < index[None, :, None])
    )
    rank = jnp.sum(ahead.astype(I32), axis=2)
    most = jnp.max(jnp.sum((by_chip > WSTART).astype(I32), axis=1))
    need = (most + 1) // 2
    level = sum((need > n).astype(I32) for n in LEVELS[:-1])

    chip = place // 2
    mine = 2 * jnp.arange(per_core, dtype=I32) + place % 2
    my_rank = jnp.sum(
        jnp.where(jnp.arange(TASKS // pair, dtype=I32)[:, None] == chip, rank, 0), axis=0
    )
    local = jnp.sum(jnp.where(my_rank[None, :] == mine[:, None], index[None, :], 0), axis=1)
    swapped = (local // per_core != place % 2).astype(I32)
    from_task = swapped * per_core + local % per_core
    operands = (
        deter, other, draws, actions, horizons, offsets, rank, local, from_task,
        embed_stoch, embed_act, w, prior_weight, logit_weight, head,
    )
    branches = [lambda args, n=n: window(n, args, holders, shards) for n in LEVELS]
    return tuple(lax.switch(level, branches, operands))


def solution(mesh):
    in_specs = (
        P("task", "mp"),
        P(None, None, "task"),
        P(None, "task"),
        P(),
        P(),
        P(),
        P(),
        P(None, None, "mp"),
        P(),
        P(),
        P(),
    )
    out_specs = (P(None, "task"), P(None, "task"), P(None, "task"), P("task", "mp"))
    return jax.shard_map(
        on_device, mesh=mesh, in_specs=in_specs, out_specs=out_specs, check_vma=False
    )
```

```python
import functools

import jax
import jax.numpy as jnp
from jax import lax
from jax.experimental import pallas as pl
from jax.experimental.pallas import tpu as pltpu
from jax.sharding import PartitionSpec as P

HID = 1024
GROUPS = 32
CLASSES = 32
TASKS = 64
BLK_DEV = 4
STEPS = 4
WSTART = 16
DEPTH = GROUPS + 1
LEVELS = (6, 8)
PIECE = 32
ROLLED = (8,)
F32 = jnp.float32
BF16 = jnp.bfloat16
I32 = jnp.int32


def silu(v):
    return v * sigmoid(v)


def sigmoid(v):
    return 0.5 + 0.5 * jnp.tanh(0.5 * v)


def row_norm(pre):
    entries = pre.shape[1]
    avg = jnp.sum(pre, axis=1, keepdims=True) / entries
    squares = jnp.sum(pre * pre, axis=1, keepdims=True) / entries
    return (pre - avg) * lax.rsqrt(squares - avg * avg + 1e-5)


def spread_matrix():
    variable = lax.broadcasted_iota(I32, (GROUPS, HID), 0)
    entry = lax.broadcasted_iota(I32, (GROUPS, HID), 1)
    return (entry // CLASSES == variable).astype(F32).astype(BF16)


def chosen_mask(by_row, spread):
    wide = jnp.dot(by_row, spread, preferred_element_type=F32)
    entry = lax.broadcasted_iota(I32, wide.shape, 1)
    return wide == (entry % CLASSES).astype(F32)


def embed_kernel(
    first, at_ref, ev_hbm, stoch_hbm, act_ref, w_hbm, out_hbm, hot_hbm,
    picks_ref, stoch_ref, wbuf, hot_ref, out_ref, sem, done_sem,
):
    steps, rows, _ = hot_ref.shape
    count = rows // PIECE

    def fetch(step, k):
        at = pl.ds(pl.multiple_of(at_ref[first + step, k], PIECE), PIECE)
        to = pl.ds(k * PIECE, PIECE)
        return pltpu.make_async_copy(
            ev_hbm.at[first + step, at], picks_ref.at[step, to], sem.at[step, k]
        )

    def give(step, q):
        ref, hbm = ((hot_ref, hot_hbm), (out_ref, out_hbm))[q]
        return pltpu.make_async_copy(ref.at[step], hbm.at[step], done_sem.at[q, step])

    def start(step, _):
        for k in range(count):
            fetch(step, k).start()
        return 0

    lax.fori_loop(0, steps, start, 0)
    table = pltpu.make_async_copy(stoch_hbm, stoch_ref, done_sem.at[2, 0])
    table.start()
    weights = pltpu.make_async_copy(w_hbm.at[:, pl.ds(0, HID), :], wbuf, done_sem.at[2, 1])
    weights.start()
    spread = spread_matrix()
    ids = lax.broadcasted_iota(I32, (rows, act_ref.shape[0]), 1).astype(F32)

    def make(step, _):
        for k in range(count):
            fetch(step, k).wait()
        wanted = picks_ref[step]
        hot = chosen_mask(wanted[:, :GROUPS], spread).astype(F32).astype(BF16)
        hot_ref[step] = hot
        give(step, 0).start()

        @pl.when(step == 0)
        def _():
            table.wait()

        action = wanted[:, GROUPS : GROUPS + 1].astype(F32)
        act_hot = (ids == action).astype(F32).astype(BF16)
        pre = jnp.dot(hot, stoch_ref[...], preferred_element_type=F32) + jnp.dot(
            act_hot, act_ref[...], preferred_element_type=F32
        )
        embedded = silu(row_norm(pre)).astype(BF16)

        @pl.when(step == 0)
        def _():
            weights.wait()

        share = wbuf.shape[2]
        for k in range(wbuf.shape[0]):
            out_ref[step, :, k * share : (k + 1) * share] = jnp.dot(
                embedded, wbuf[k], preferred_element_type=F32
            )
        give(step, 1).start()
        return 0

    lax.fori_loop(0, steps, make, 0)

    def finish(step, _):
        give(step, 0).wait()
        give(step, 1).wait()
        return 0

    lax.fori_loop(0, steps, finish, 0)


def full_lanes(part):
    rows = part.shape[0]
    if rows < 256:
        part = jnp.concatenate([part, jnp.zeros((256 - rows, 128), F32)], axis=0)
    return jnp.transpose(part)


def lanes_from_row(row, rows):
    return jnp.transpose(jnp.broadcast_to(row, (128, row.shape[1])))[:rows]


def gates_kernel(step, emb_hbm, x_hbm, w_ref, g_ref, stat_ref, x_ref, wbuf, sem):
    parts, depth, share = w_ref.shape
    chunks = depth // HID - 1
    per = HID // share

    def fetch(c):
        at = pl.ds(pl.multiple_of((c + 1) * HID, HID), HID)
        return pltpu.make_async_copy(w_ref.at[:, at, :], wbuf.at[c], sem.at[c])

    def fetch_x(c):
        at = pl.ds(c * per, per)
        return pltpu.make_async_copy(x_hbm.at[at], x_ref.at[at], sem.at[chunks + c])

    emb = pltpu.make_async_copy(emb_hbm.at[step], g_ref, sem.at[2 * chunks])
    fetch_x(0).start()
    fetch(0).start()
    emb.start()
    for c in range(1, chunks):
        fetch_x(c).start()
        fetch(c).start()
    emb.wait()

    def add(c, _):
        fetch_x(c).wait()
        left = jnp.concatenate([x_ref[c * per + q] for q in range(per)], axis=1)
        fetch(c).wait()
        for k in range(parts):
            g_ref[:, k * share : (k + 1) * share] += jnp.dot(
                left, wbuf[c, k], preferred_element_type=F32
            )
        return 0

    lax.fori_loop(0, chunks, add, 0)
    rows, width = g_ref.shape
    part = jnp.zeros((rows, 128), F32)
    part_sq = part
    for q in range(width // 128):
        piece = g_ref[:, q * 128 : (q + 1) * 128]
        part += piece
        part_sq += piece * piece
    sums = jnp.concatenate(
        [
            jnp.sum(full_lanes(part), axis=0, keepdims=True),
            jnp.sum(full_lanes(part_sq), axis=0, keepdims=True),
        ],
        axis=0,
    )
    for q in range(stat_ref.shape[0]):
        stat_ref[q] = sums


def spread_copies(low_ref, low_hbm, rows, sem):
    for k in range(low_hbm.shape[0]):
        pltpu.make_async_copy(low_ref.at[rows], low_hbm.at[k, rows], sem.at[k]).start()


def update_kernel(entries, step, g_ref, stat_ref, carried_ref, live_ref, new_ref, low_ref):
    sums = jnp.sum(stat_ref[...], axis=0) / entries
    avg = sums[0:1]
    inv = lax.rsqrt(sums[1:2] - avg * avg + 1e-5)
    rows, share = carried_ref.shape
    avg_l = lanes_from_row(avg, rows)
    inv_l = lanes_from_row(inv, rows)
    live_l = lanes_from_row(live_ref[pl.ds(step, 1), :], rows)
    for q in range(share // 128):
        def normed(part):
            at = part * share + q * 128
            return (g_ref[:, at : at + 128] - avg_l) * inv_l

        held = carried_ref[:, q * 128 : (q + 1) * 128]
        reset = sigmoid(normed(0))
        candidate = jnp.tanh(reset * normed(1))
        update = sigmoid(normed(2) - 1.0)
        renewed = update * candidate + (1.0 - update) * held
        renewed = jnp.where(live_l > 0, renewed, held)
        new_ref[:, q * 128 : (q + 1) * 128] = renewed
        low = renewed.astype(BF16)
        for k in range(low_ref.shape[0]):
            low_ref[k, :, q * 128 : (q + 1) * 128] = low


def two_parts(values):
    high = values.astype(BF16)
    return high, (values - high.astype(F32)).astype(BF16)


def prior_kernel(
    at_step, step, x_hbm, w_ref, logit_ref, head_ref, hot_hbm, live_ref, out_ref,
    x_ref, wbuf, lbuf, pre_ref, hid_ref, hot_ref, parts_ref, sem,
):
    shards, rows, share = x_ref.shape
    chunks = w_ref.shape[0] // HID
    per = HID // share

    def fetch(c):
        at = pl.ds(pl.multiple_of(c * HID, HID), HID)
        return pltpu.make_async_copy(w_ref.at[at], wbuf.at[c], sem.at[c])

    state = pltpu.make_async_copy(x_hbm, x_ref, sem.at[chunks + 2])
    state.start()
    for c in range(chunks):
        fetch(c).start()
    last = pltpu.make_async_copy(logit_ref, lbuf, sem.at[chunks])
    last.start()
    marks = pltpu.make_async_copy(hot_hbm.at[at_step], hot_ref, sem.at[chunks + 1])
    marks.start()
    pre_ref[...] = jnp.zeros(pre_ref.shape, F32)
    state.wait()

    def add(c, _):
        left = jnp.concatenate([x_ref[c * per + q] for q in range(per)], axis=1)
        fetch(c).wait()
        pre_ref[...] += jnp.dot(left, wbuf[c], preferred_element_type=F32)
        return 0

    lax.fori_loop(0, chunks, add, 0)

    def squash(k, _):
        at = pl.ds(pl.multiple_of(k * PIECE, PIECE), PIECE)
        hid_ref[at] = silu(row_norm(pre_ref[at])).astype(BF16)
        return 0

    lax.fori_loop(0, rows // PIECE, squash, 0)
    last.wait()
    marks.wait()
    across = (((1,), (1,)), ((), ()))
    heads = lax.dot_general(head_ref[...], hid_ref[...], across, preferred_element_type=F32)
    pre_ref[...] = jnp.dot(hid_ref[...], lbuf[...], preferred_element_type=F32)
    spread = spread_matrix()

    def classes(k, _):
        at = pl.ds(pl.multiple_of(k * PIECE, PIECE), PIECE)
        high, low = two_parts(jnp.exp(5.0 * jnp.tanh(pre_ref[at] / 5.0)))
        hot = hot_ref[at]
        parts_ref[0, at] = high
        parts_ref[1, at] = low
        parts_ref[2, at] = high * hot
        parts_ref[3, at] = low * hot
        return 0

    lax.fori_loop(0, rows // PIECE, classes, 0)

    def over_groups(k):
        return lax.dot_general(
            spread, parts_ref[k], across, preferred_element_type=F32
        ) + lax.dot_general(spread, parts_ref[k + 1], across, preferred_element_type=F32)

    chances = 0.99 * over_groups(2) / over_groups(0) + 0.01 / CLASSES
    log_prob = jnp.sum(jnp.log(chances), axis=0, keepdims=True)
    live = live_ref[pl.ds(step, 1), :rows]
    out_ref[...] = jnp.zeros(out_ref.shape, F32)
    out_ref[0:1, :rows] = log_prob * live
    out_ref[1:2, :rows] = heads[0:1] * live
    out_ref[2:3, :rows] = sigmoid(heads[1:2]) * live


def pick_kernel(at_ref, own_ref, other_ref, carried_ref, low_hbm, *refs):
    *rest, low_ref, sem = refs
    count, per_task, share = own_ref.shape
    done = carried_ref.shape[0] // per_task
    for i in range(count):
        at = at_ref[i]
        inner = at % count
        value = jnp.where(at < count, own_ref[inner], other_ref[inner])
        low = value.astype(BF16)
        rows = slice(i * per_task, (i + 1) * per_task)
        if i < done:
            carried_ref[rows] = value
            low_ref[rows] = low
        else:
            rest[0][(i - done) * per_task : (i - done + 1) * per_task] = low
        if i == done - 1:
            spread_copies(low_ref, low_hbm, pl.ds(0, done * per_task), sem)
    for k in range(low_hbm.shape[0]):
        pltpu.make_async_copy(low_ref, low_hbm.at[k], sem.at[k]).wait()


def settle_kernel(
    rows, at_ref, to_ref, got_ref, left_ref, outs_ref,
    log_ref, reward_ref, cont_ref, final_ref, buf, tall_ref, mine_ref, sem,
):
    count, per_task, share = buf.shape
    done = rows // per_task
    for i in range(count):
        chunk = at_ref[1, i]

        def bring(ref, chunk, i=i):
            at = pl.ds(pl.multiple_of(chunk * per_task, per_task), per_task)
            pltpu.make_async_copy(ref.at[at_ref[0, i], at], buf.at[i], sem.at[i]).start()

        if done == count:
            bring(got_ref, chunk)
        else:
            pl.when(chunk < done)(functools.partial(bring, got_ref, chunk))
            pl.when(chunk >= done)(functools.partial(bring, left_ref, chunk - done))

    holders, depth, lanes = outs_ref.shape
    half = depth // 2
    for d in range(holders):
        both = outs_ref[d].astype(F32)
        tall_ref[d * lanes : (d + 1) * lanes] = jnp.transpose(both[:half] + both[half:])
    for t in range(STEPS):
        for i in range(count):
            at = to_ref[t, i]
            from_rows = pl.ds(pl.multiple_of(jnp.maximum(at, 0), per_task), per_task)
            mine_ref[i * per_task : (i + 1) * per_task] = jnp.where(at >= 0, tall_ref[from_rows], 0.0)
        flat = jnp.transpose(mine_ref[...])
        for k, ref in enumerate((log_ref, reward_ref, cont_ref)):
            ref[t : t + 1] = flat[t * 3 + k : t * 3 + k + 1]
    for i in range(count):
        pltpu.make_async_copy(got_ref.at[0, pl.ds(0, per_task)], buf.at[i], sem.at[i]).wait()
        final_ref[i * per_task : (i + 1) * per_task] = buf[i].astype(F32)


def params(mib):
    return pltpu.CompilerParams(vmem_limit_bytes=mib * 1024 * 1024)


WHOLE = pl.BlockSpec()
STAY = pl.BlockSpec(memory_space=pltpu.HBM)
EITHER = pl.BlockSpec(memory_space=pl.ANY)
SCALARS = pl.BlockSpec(memory_space=pltpu.SMEM)


def placed(specs, operands):
    return tuple(
        pltpu.with_memory_space_constraint(o, pltpu.HBM) if s is STAY else o
        for s, o in zip(specs, operands, strict=True)
    )


def embed(first, steps, at, everyone, stoch, act, w, rows):
    depth = everyone.shape[2]
    parts, _, share = w.shape
    specs = [SCALARS, STAY, STAY, WHOLE, STAY]
    return pl.pallas_call(
        functools.partial(embed_kernel, first),
        in_specs=specs,
        out_specs=[STAY, STAY],
        out_shape=[
            pltpu.HBM((steps, rows, parts * share), F32),
            pltpu.HBM((steps, rows, HID), BF16),
        ],
        scratch_shapes=[
            pltpu.VMEM((steps, rows, depth), BF16),
            pltpu.VMEM(stoch.shape, BF16),
            pltpu.VMEM((parts, HID, share), BF16),
            pltpu.VMEM((steps, rows, HID), BF16),
            pltpu.VMEM((steps, rows, parts * share), F32),
            pltpu.SemaphoreType.DMA((steps, rows // PIECE)),
            pltpu.SemaphoreType.DMA((3, max(steps, 2))),
        ],
        compiler_params=params(24),
        name="embed",
    )(*placed(specs, (at, everyone, stoch, act, w)))


def stepped(kernel, steps, specs, operands):
    operands = placed(specs, operands)
    if all(isinstance(step, int) for step in steps):
        return functools.partial(kernel, *steps), specs, operands

    def with_scalars(step_ref, *refs):
        kernel(*(step_ref[k] for k in range(len(steps))), *refs)

    return with_scalars, [SCALARS, *specs], (jnp.stack(steps), *operands)


def gates(at, emb, x, w):
    kernel, specs, operands = stepped(gates_kernel, (at,), [STAY, EITHER, STAY], (emb, x, w))
    shards, rows, share = x.shape
    parts, depth, _ = w.shape
    return pl.pallas_call(
        kernel,
        in_specs=specs,
        out_shape=[
            jax.ShapeDtypeStruct((rows, parts * share), F32),
            jax.ShapeDtypeStruct((shards, 2, 256), F32),
        ],
        scratch_shapes=[
            pltpu.VMEM(x.shape, BF16),
            pltpu.VMEM((depth // HID - 1, parts, HID, share), BF16),
            pltpu.SemaphoreType.DMA((2 * (depth // HID) - 1,)),
        ],
        compiler_params=params(24),
        name="gates",
    )(*operands)


def renew(moment, g, stats, carried, live, entries, copies):
    kernel, specs, operands = stepped(
        functools.partial(update_kernel, entries), (moment,), [WHOLE] * 4, (g, stats, carried, live)
    )
    rows, share = carried.shape
    return pl.pallas_call(
        kernel,
        in_specs=specs,
        out_shape=[
            jax.ShapeDtypeStruct((rows, share), F32),
            jax.ShapeDtypeStruct((copies, rows, share), BF16),
        ],
        compiler_params=params(16),
        name="renew",
    )(*operands)


def prior(at, moment, x, w, logit, head, hot, live):
    kernel, specs, operands = stepped(
        prior_kernel,
        (at, moment),
        [STAY, STAY, STAY, WHOLE, STAY, WHOLE],
        (x, w, logit, head, hot, live),
    )
    rows = x.shape[1]
    chunks = w.shape[0] // HID
    return pl.pallas_call(
        kernel,
        in_specs=specs,
        out_shape=jax.ShapeDtypeStruct((8, 256), F32),
        scratch_shapes=[
            pltpu.VMEM(x.shape, BF16),
            pltpu.VMEM((chunks, HID, HID), BF16),
            pltpu.VMEM((HID, HID), BF16),
            pltpu.VMEM((rows, HID), F32),
            pltpu.VMEM((rows, HID), BF16),
            pltpu.VMEM((rows, HID), BF16),
            pltpu.VMEM((4, rows, HID), BF16),
            pltpu.SemaphoreType.DMA((chunks + 3,)),
        ],
        compiler_params=params(28),
        name="prior",
    )(*operands)


def pick(at, own, other, rows, shards):
    count, per_task, share = own.shape
    left = count * per_task - rows
    shapes = [
        jax.ShapeDtypeStruct((rows, share), F32),
        pltpu.HBM((shards, rows, share), BF16),
    ]
    if left:
        shapes.append(jax.ShapeDtypeStruct((left, share), BF16))
    return pl.pallas_call(
        pick_kernel,
        in_specs=[SCALARS, WHOLE, WHOLE],
        out_shape=shapes,
        out_specs=[WHOLE, STAY] + [WHOLE] * (len(shapes) - 2),
        scratch_shapes=[pltpu.VMEM((rows, share), BF16), pltpu.SemaphoreType.DMA((shards,))],
        compiler_params=params(16),
        name="pick",
    )(at, own, other)


def settle(at, to, got, left, outs, rows, count, per_task):
    share = got.shape[2]
    holders, depth, lanes = outs.shape
    return pl.pallas_call(
        functools.partial(settle_kernel, rows),
        in_specs=[SCALARS, SCALARS, EITHER, EITHER, WHOLE],
        out_shape=[jax.ShapeDtypeStruct((STEPS, count * per_task), F32)] * 3
        + [jax.ShapeDtypeStruct((count * per_task, share), F32)],
        scratch_shapes=[
            pltpu.VMEM((count, per_task, share), BF16),
            pltpu.VMEM((holders * lanes, depth // 2), F32),
            pltpu.VMEM((count * per_task, depth // 2), F32),
            pltpu.SemaphoreType.DMA((count,)),
        ],
        compiler_params=params(16),
        name="settle",
    )(at, to, got, left, outs)


def exchange(copies, axis):
    return lax.all_to_all(copies, axis, 0, 0, tiled=True)


def window(count, args, holders, shards):
    (
        deter, other, draws, actions, horizons, offsets, rank, local, from_task,
        stoch, act, w, prior_weight, logit, head,
    ) = args
    all_rows, share = deter.shape
    per_core = local.shape[0]
    per_task = all_rows // per_core
    rows = count * per_task
    entries = 3 * share * shards
    place = lax.axis_index("task")
    pair = 2 * per_core
    in_block = per_core // BLK_DEV

    carried, low, *rest = pick(
        from_task,
        deter.reshape(per_core, per_task, share),
        other.reshape(per_core, per_task, share),
        rows,
        shards,
    )
    x = exchange(low, "mp")

    sent = jnp.concatenate([draws, actions[:, None]], axis=1).astype(BF16)
    sent = jnp.concatenate([sent.reshape(STEPS * DEPTH, all_rows), *rest], axis=0)
    everyone = lax.all_gather(sent, "task")
    left = everyone[:, STEPS * DEPTH :]
    everyone = everyone[:, : STEPS * DEPTH].reshape(holders, STEPS, DEPTH, all_rows)
    everyone = jnp.transpose(everyone, (1, 0, 3, 2)).reshape(STEPS, holders * all_rows, DEPTH)

    task = place // 2 * pair + local
    horizon = jnp.sum(
        jnp.where(task[:, None] == jnp.arange(TASKS, dtype=I32)[None, :], horizons[None, :], 0), axis=1
    )
    moments = WSTART + jnp.arange(STEPS, dtype=I32)
    living = jnp.repeat((horizon[None, :] > moments[:, None]).astype(F32), per_task, axis=1)

    running = jnp.cumsum(offsets, axis=0) % holders
    lane_block = task % per_core // in_block
    blocks = jnp.arange(BLK_DEV, dtype=I32)
    ahead_by = jnp.sum(
        jnp.where(lane_block[None, :, None] == blocks, running[:, None, :], 0), axis=2
    )
    slot = (task[None, :] // per_core + ahead_by) % holders
    source = slot * all_rows + (task % per_core)[None, :] * per_task
    first = STEPS if count in ROLLED else 1
    emb, hot = embed(0, first, source, everyone, stoch, act, w, rows)
    x, emb, hot = lax.optimization_barrier((x, emb, hot))

    held = jnp.repeat((place - running) % holders, in_block, axis=1) * per_core
    held = held + jnp.arange(per_core, dtype=I32)[None, :]
    dealt = jnp.sum(
        jnp.where(held[:, :, None] == jnp.arange(TASKS, dtype=I32), rank.reshape(-1), 0), axis=2
    )
    core = held // pair * 2 + dealt % 2
    chunk = dealt // 2
    settle_at = jnp.stack([core[STEPS - 1], chunk[STEPS - 1]])
    to = jnp.where(chunk < count, core * share + chunk * per_task, -1)

    def likely(at, moment, x, hot):
        return prior(at, moment, x, prior_weight, logit, head, hot, living)[:3]

    def gated(at, moment, x, emb, carried):
        g, stats = gates(at, emb, x, w)
        stats = exchange(stats, "mp")
        return renew(moment, g, stats, carried, living, entries, shards)

    small = []
    if count in ROLLED:

        def body(state, moment):
            x, carried = state
            carried, low = gated(moment, moment, x, emb, carried)
            out = likely(moment, moment, x, hot)
            x, out = lax.optimization_barrier((exchange(low, "mp"), out))
            return (x, carried), out

        (x, carried), outs = lax.scan(body, (x, carried), jnp.arange(STEPS - 1, dtype=I32))
        small.append(outs.reshape(-1, outs.shape[2]))
        at = STEPS - 1
    else:
        at = 0
        for moment in range(STEPS - 1):
            carried, low = gated(at, moment, x, emb, carried)
            out = likely(at, moment, x, hot)
            if moment == 0:
                emb, hot = embed(1, STEPS - 1, source, everyone, stoch, act, w, rows)
            x = exchange(low, "mp")
            x, out, emb, hot, left = lax.optimization_barrier((x, out, emb, hot, left))
            small.append(out)
            at = moment

    g, stats = gates(at, emb, x, w)
    stats = exchange(stats, "mp")
    out = likely(at, STEPS - 1, x, hot)
    stats, small, out = lax.optimization_barrier((stats, small, out))
    _, low = renew(STEPS - 1, g, stats, carried, living, entries, 1)

    outs = jnp.concatenate([*small, out], axis=0)
    high, low_part = two_parts(outs)
    pad = jnp.zeros((16 - high.shape[0], share), BF16)
    sent = jnp.concatenate([low[0], high, pad, low_part, pad], axis=0)
    if count in ROLLED:
        got = exchange(jnp.broadcast_to(sent[None], (holders, *sent.shape)), "task")
    else:
        got = lax.all_gather(sent, "task")
    outs = got[:, rows:]
    if not rest:
        left = got
    return settle(settle_at, to, got, left, outs, rows, per_core, per_task)


def on_device(
    deter,
    draws,
    actions,
    horizons,
    offsets,
    embed_stoch,
    embed_act,
    gru_weight,
    prior_weight,
    logit_weight,
    head_weight,
):
    holders = lax.axis_size("task")
    place = lax.axis_index("task")
    shards = lax.axis_size("mp")
    rows, share = deter.shape
    per_core = TASKS // holders
    pair = 2 * per_core

    other = lax.ppermute(deter, "task", [(i, i ^ 1) for i in range(holders)])
    w = jnp.transpose(gru_weight, (1, 0, 2))
    head = jnp.transpose(head_weight)

    by_chip = horizons.reshape(TASKS // pair, pair)
    index = jnp.arange(pair, dtype=I32)
    ahead = (by_chip[:, None, :] > by_chip[:, :, None]) | (
        (by_chip[:, None, :] == by_chip[:, :, None]) & (index[None, None, :] < index[None, :, None])
    )
    rank = jnp.sum(ahead.astype(I32), axis=2)
    most = jnp.max(jnp.sum((by_chip > WSTART).astype(I32), axis=1))
    need = (most + 1) // 2
    level = sum((need > n).astype(I32) for n in LEVELS[:-1])

    chip = place // 2
    mine = 2 * jnp.arange(per_core, dtype=I32) + place % 2
    my_rank = jnp.sum(
        jnp.where(jnp.arange(TASKS // pair, dtype=I32)[:, None] == chip, rank, 0), axis=0
    )
    local = jnp.sum(jnp.where(my_rank[None, :] == mine[:, None], index[None, :], 0), axis=1)
    swapped = (local // per_core != place % 2).astype(I32)
    from_task = swapped * per_core + local % per_core
    operands = (
        deter, other, draws, actions, horizons, offsets, rank, local, from_task,
        embed_stoch, embed_act, w, prior_weight, logit_weight, head,
    )
    branches = [lambda args, n=n: window(n, args, holders, shards) for n in LEVELS]
    return tuple(lax.switch(level, branches, operands))


def solution(mesh):
    in_specs = (
        P("task", "mp"),
        P(None, None, "task"),
        P(None, "task"),
        P(),
        P(),
        P(),
        P(),
        P(None, None, "mp"),
        P(),
        P(),
        P(),
    )
    out_specs = (P(None, "task"), P(None, "task"), P(None, "task"), P("task", "mp"))
    return jax.shard_map(
        on_device, mesh=mesh, in_specs=in_specs, out_specs=out_specs, check_vma=False
    )
```
